512 devices in a mesh: dp: 32 (over y, x, core), ctx: 16 (over z).
Axes of the slice: x: 4, y: 4, z: 16, core: 2. Of those that a mesh axis runs over, the one named last changes fastest.
Arguments:
- q_src: bfloat16 [65536, 4096], P(('dp', 'ctx')), may hold values from -40 to 40
- kv_src: bfloat16 [65536, 1024], P(('dp', 'ctx')), may hold values from -40 to 40
- route: int32 [65536, 1], replicated, may hold values from 0 to 31; in each aligned block of 2048 rows (0 to 2047, 2048 to 4095, ...) at most 96 rows name the same one
- doc_ids: int32 [32, 3072], P('dp'), may hold values from 0 to 5, never falling along the last dimension, each value on 1 to 1024 neighbouring positions
Outputs:
- attended: bfloat16 [98304, 4096], P(('dp', 'ctx'))
The draws below stay inside these ranges and needn't reach their ends.
Inputs may be any that keep to these rules, and one draw needn't show every extreme that they name: `route`: within each source group's 2048 rows (aligned blocks of 2048 rows), no sequence is named by more than 96 rows, a bound that some block reaches. `doc_ids`: never falling along a sequence; every document has 1 to 1024 slots and one has exactly 1024.
All inputs are finite; a program needn't handle non-finite values.
Results may differ from the reference program's by a relative error of at most 0.011.
Values may be sent and summed in bfloat16 or wider, within the bound.
A program may use at most 64 MiB of HBM per device.

```python
import math
import jax
import jax.numpy as jnp
import numpy as np
from jax import lax

Q_HEADS = 32
KV_HEADS = 4
HEAD_DIM = 128
SEQS = 32
L = 2048
CAP = 96
PACK = 3072
DOC_MOST = 1024
DOCS = 6


def draw_q_src(key, part):
    row_count = SEQS * L
    group_size = Q_HEADS // KV_HEADS
    base_draw = jax.random.normal(jax.random.fold_in(key, 1), (row_count, KV_HEADS, group_size, HEAD_DIM), jnp.float32)
    base_draw = jnp.clip(base_draw, -5.0, 5.0)
    return jnp.clip(base_draw, -40.0, 40.0).reshape(row_count, Q_HEADS * HEAD_DIM).astype(jnp.bfloat16)


def draw_kv_src(key, part):
    row_count = SEQS * L
    base_draw = jax.random.normal(jax.random.fold_in(key, 5), (row_count, 2, KV_HEADS, HEAD_DIM), jnp.float32)
    base_draw = jnp.clip(base_draw, -5.0, 5.0)
    return jnp.clip(base_draw, -40.0, 40.0).reshape(row_count, 2 * KV_HEADS * HEAD_DIM).astype(jnp.bfloat16)


def profile(number_of, total, bound, slope):
    weights = [(1 << 20) // math.isqrt(grade ** slope) + 1 for grade in range(2, number_of + 1)]
    surplus, counts = total - bound - (number_of - 1), [1] * (number_of - 1)
    while surplus > 0:
        free = [i for i in range(number_of - 1) if counts[i] < bound]
        pool, remaining = sum([weights[i] for i in free]), surplus
        for i in free:
            extra = min(bound - counts[i], max(1, remaining * weights[i] // pool), surplus)
            counts[i] = counts[i] + extra
            surplus = surplus - extra
    return np.array([bound] + counts)


def ragged(own_key, number_of, total, most, slope):
    if number_of == 2:
        one = jax.random.randint(own_key, (), max(1, total - most), min(most, total - 1) + 1)
        return jnp.stack([one, total - one])
    sizes = jnp.asarray(profile(number_of, total, most, slope), jnp.int32)
    pairs = (number_of - 1) // 2
    source_of, sink = sizes[1:1 + 2 * pairs:2], sizes[2:2 + 2 * pairs:2]
    slack = jnp.minimum(source_of - 1, most - sink)
    moved = jax.random.randint(jax.random.fold_in(own_key, 1), (pairs,), 0, 1 << 20) % (slack + 1)
    sizes = sizes.at[1:1 + 2 * pairs:2].set(source_of - moved).at[2:2 + 2 * pairs:2].set(sink + moved)
    return sizes[jax.random.permutation(jax.random.fold_in(own_key, 2), number_of)]


def routed_block(rng, own, number, rows, amount, top, bound, skew):
    sequence = jax.random.permutation(rng, amount)
    crowded, usual = shares(amount, rows * top, bound, skew, True), shares(amount, rows * top, bound, skew, False)
    places = jnp.arange(amount)

    def named(tallies, rotation):
        used = int((tallies > 0).sum())
        fixed = max(1, used // 4)
        shifted = fixed + (places - fixed + rotation * (used - fixed)) % max(1, amount - fixed)
        return jnp.zeros((amount,), jnp.int32).at[sequence[jnp.where(places < fixed, places, shifted)]].set(jnp.asarray(tallies, jnp.int32))

    tallies = jnp.where(number % 4 == 0, named(crowded, number // 4), named(usual, number - number // 4 - 1))
    mixed = jax.random.permutation(jax.random.fold_in(own, 3), amount)
    giver, sink = mixed[0:amount // 2 * 2:2], mixed[1:amount // 2 * 2:2]
    room = jnp.minimum(tallies[giver] - 1, bound - tallies[sink]) // 2
    room = jnp.where((giver == sequence[0]) | (sink == sequence[0]) | (tallies[sink] == 0), 0, jnp.maximum(room, 0))
    shifted = jax.random.randint(jax.random.fold_in(own, 4), (amount // 2,), 0, 1 << 20) % (room + 1)
    tallies = tallies.at[giver].add(-shifted).at[sink].add(shifted)
    labels = jnp.searchsorted(jnp.cumsum(tallies), jnp.arange(rows * top), side="right").astype(jnp.int32)
    grid = labels.reshape(top, rows).T
    grid = grid[jax.random.permutation(jax.random.fold_in(own, 1), rows)]
    rotation = jax.random.randint(jax.random.fold_in(own, 2), (rows, 1), 0, top)
    return jnp.take_along_axis(grid, (jnp.arange(top)[None, :] + rotation) % top, axis=1)


def shares(count, total, most, skew, full):
    loads = [(1 << 20) // math.isqrt(rank ** skew) + 1 for rank in range(1, count + 1)]
    largest = most if full else min(most, max(-(-total // count), total * loads[0] // sum(loads)))
    least = 1 if total - largest >= count - 1 else 0
    holding, spare = [largest] + [least] * (count - 1), total - largest - least * (count - 1)
    while spare > 0:
        free = [i for i in range(1, count) if holding[i] < largest] or [i for i in range(1, count) if holding[i] < most]
        whole, left = sum([loads[i] for i in free]), spare
        for i in free:
            extra = min(most - holding[i], max(1, left * loads[i] // whole), spare)
            holding[i] = holding[i] + extra
            spare = spare - extra
    return np.array(holding)


def setup_inputs(seed: int = 0) -> dict:
    splits = jax.random.split(jax.random.key(seed), 5)
    q_src = draw_q_src(jax.random.fold_in(splits[4], 71), 0)
    kv_src = draw_kv_src(jax.random.fold_in(splits[4], 71), 0)
    route_keys = jax.random.split(jax.random.fold_in(splits[2], 1), (SEQS * L) // L)
    route_turns = jax.random.permutation(jax.random.fold_in(splits[2], 3), (SEQS * L) // L)
    route = jax.vmap(lambda own, number: routed_block(jax.random.fold_in(splits[2], 2), own, number, L, SEQS, 1, CAP, 1))(route_keys, route_turns).reshape((SEQS * L, 1))
    doc_ids = jax.vmap(lambda own: jnp.searchsorted(jnp.cumsum(ragged(own, DOCS, PACK, DOC_MOST, 2)), jnp.arange(PACK), side="right"))(jax.random.split(splits[3], SEQS)).reshape((SEQS, PACK)).astype(jnp.int32)
    return {"q_src": q_src, "kv_src": kv_src, "route": route, "doc_ids": doc_ids}


def attend(queries, kv_pairs, doc_rows, live_rows, kv_local):
    pack_len = queries.shape[0]
    head_count = queries.shape[1] // HEAD_DIM
    group_size = head_count // kv_local
    block_len = math.gcd(pack_len, 512)
    window = min(pack_len, DOC_MOST + block_len)
    score_scale = HEAD_DIM ** -0.5
    grouped = queries.reshape(pack_len, kv_local, group_size, HEAD_DIM)
    split_pairs = kv_pairs.reshape(pack_len, 2, kv_local, HEAD_DIM)

    def one_block(block_index):
        row_start = block_index * block_len
        key_start = jnp.maximum(row_start + block_len - window, 0)
        query_block = lax.dynamic_slice_in_dim(grouped, row_start, block_len, 0).astype(jnp.float32)
        key_block = lax.dynamic_slice_in_dim(split_pairs, key_start, window, 0).astype(jnp.float32)
        query_docs = lax.dynamic_slice_in_dim(doc_rows, row_start, block_len, 0)
        key_docs = lax.dynamic_slice_in_dim(doc_rows, key_start, window, 0)
        query_pos = row_start + jnp.arange(block_len, dtype=jnp.int32)
        key_pos = key_start + jnp.arange(window, dtype=jnp.int32)
        allowed = (query_docs[:, None] == key_docs[None, :]) & (key_pos[None, :] <= query_pos[:, None])
        scores = jnp.einsum("qkgd,skd->kgqs", query_block, key_block[:, 0]) * score_scale
        masked = jnp.where(allowed, scores, -1e30)
        row_max = jnp.max(masked, axis=-1, keepdims=True)
        exponent = jnp.where(allowed, jnp.exp(masked - row_max), 0.0)
        probs = exponent / jnp.sum(exponent, axis=-1, keepdims=True)
        weights = probs.astype(jnp.bfloat16)
        mixed = jnp.einsum("kgqs,skd->qkgd", weights.astype(jnp.float32), key_block[:, 1])
        mixed = jnp.where((query_pos < live_rows)[:, None, None, None], mixed, 0.0)
        return mixed.astype(jnp.bfloat16).reshape(block_len, head_count * HEAD_DIM)

    blocks = lax.map(one_block, jnp.arange(pack_len // block_len, dtype=jnp.int32))
    return blocks.reshape(pack_len, head_count * HEAD_DIM)


def reference(q_src, kv_src, route, doc_ids):
    plan_rows = route.reshape(-1).astype(jnp.int32)
    seq_ids = jnp.arange(SEQS, dtype=jnp.int32)
    onehot = (plan_rows[:, None] == seq_ids[None, :]).astype(jnp.int32)
    before = (jnp.cumsum(onehot, axis=0) - onehot).astype(jnp.int32)
    position = jnp.sum(before * onehot, axis=1).astype(jnp.int32)
    totals = jnp.sum(onehot, axis=0).astype(jnp.int32)
    flat_slot = (plan_rows * PACK + position).astype(jnp.int32)
    packed_q = jnp.zeros((SEQS * PACK, q_src.shape[1]), jnp.bfloat16).at[flat_slot].set(q_src)
    packed_kv = jnp.zeros((SEQS * PACK, kv_src.shape[1]), jnp.bfloat16).at[flat_slot].set(kv_src)

    def per_sequence(items):
        seq_q, seq_kv, seq_docs, live_rows = items
        return attend(seq_q, seq_kv, seq_docs, live_rows, KV_HEADS)

    result = lax.map(per_sequence, (packed_q.reshape(SEQS, PACK, -1), packed_kv.reshape(SEQS, PACK, -1), doc_ids, totals))
    return result.reshape(SEQS * PACK, Q_HEADS * HEAD_DIM)
```

```python
import functools

import jax
import jax.numpy as jnp
from jax import lax
from jax.experimental import pallas as pl
from jax.experimental.pallas import tpu as pltpu
from jax.sharding import PartitionSpec as P

Q_HEADS = 32
KV_HEADS = 4
HEAD_DIM = 128
DOC_MOST = 1024
BLOCK = 256
BATCH = 4
NEG = -1e30
MESH = pl.DeviceIdType.MESH
BF16 = jnp.bfloat16
F32 = jnp.float32
I32 = jnp.int32


class Sizes:
    def __init__(self, dp, ctx, rows, cap, heads, kv_heads, doc_most, block):
        self.dp, self.ctx, self.rows, self.cap = dp, ctx, rows, cap
        self.heads, self.kv_heads = heads, kv_heads
        self.local = heads // ctx
        self.team = ctx // kv_heads
        self.group = rows * ctx
        self.pack = dp * cap
        self.slots = self.pack // ctx
        self.part = rows // self.team
        self.lanes = self.group // 128
        self.tiles = self.pack // 128
        self.doc_most, self.block = doc_most, block
        self.blocks = self.pack // block
        self.window = doc_most + block
        self.batches = dp // BATCH


def iota(shape, dim):
    return lax.broadcasted_iota(I32, shape, dim)


def alternating(n):
    order = []
    for k in range(1, n // 2):
        order += [k, n - k]
    return order + [n // 2]


def kernel(
    z, route_ref, doc_ref, q_hbm, kv_hbm, out_ref,
    qg, kvg, send_q, send_kv, recv_q, recv_kv, pq, pkv, ob, pick, place,
    target, pos, key_doc, query_doc, live_col,
    zq_s, zq_r, k1_s, k1_r, k2_s, k2_r, dkv_s, dkv_r, dq_s, dq_r, o_s, o_r, own,
):
    g = lax.axis_index("dp")
    c = lax.axis_index("ctx")
    nz, nd, hd = z.ctx, z.dp, HEAD_DIM
    quarter = lax.rem(c, z.team)
    quad = c - quarter

    barrier = pltpu.get_barrier_semaphore()

    def greet(axis, me, n):
        def body(k, _):
            pl.semaphore_signal(
                barrier, inc=1, device_id={axis: lax.rem(me + k, n)}, device_id_type=MESH
            )
            return 0

        lax.fori_loop(1, n, body, 0)

    greet("ctx", c, nz)
    greet("dp", g, nd)
    pl.semaphore_wait(barrier, nz + nd - 2)

    def remote(src, dst, s, r, axis, peer):
        return pltpu.make_async_remote_copy(
            src_ref=src, dst_ref=dst, send_sem=s, recv_sem=r,
            device_id={axis: peer}, device_id_type=MESH,
        )

    def kv_cut(half, peer):
        part = lax.rem(peer, z.team)
        head = peer // z.team
        rows = pl.ds(pl.multiple_of(part * z.part, z.part), z.part)
        cols = pl.ds(pl.multiple_of((half * z.kv_heads + head) * hd, hd), hd)
        return kv_hbm.at[rows, cols], part

    def kv_one(half, peer):
        src, part = kv_cut(half, peer)
        dst = kvg.at[c, part, :, pl.ds(half * hd, hd)]
        return remote(src, dst, k1_s.at[half, peer], k1_r.at[half, c], "ctx", peer)

    def kv_one_in(half, peer):
        dst = kvg.at[peer, quarter, :, pl.ds(half * hd, hd)]
        return remote(dst, dst, k1_s.at[half, peer], k1_r.at[half, peer], "ctx", peer)

    def kv_own(half):
        src, part = kv_cut(half, c)
        return pltpu.make_async_copy(
            src, kvg.at[c, part, :, pl.ds(half * hd, hd)], own.at[half]
        )

    def q_cut(e, peer):
        return q_hbm.at[:, pl.ds(pl.multiple_of((peer * z.local + e) * hd, hd), hd)]

    def q_one(e, peer):
        return remote(q_cut(e, peer), qg.at[e, c], zq_s.at[e, peer], zq_r.at[e, c], "ctx", peer)

    def q_one_in(e, peer):
        dst = qg.at[e, peer]
        return remote(dst, dst, zq_s.at[e, peer], zq_r.at[e, peer], "ctx", peer)

    def q_own(e):
        return pltpu.make_async_copy(q_cut(e, c), qg.at[e, c], own.at[2 + e])

    def peers(n, me):
        return [lax.rem(me + k, n) for k in alternating(n)]

    for peer in peers(nz, c):
        for half in range(2):
            kv_one(half, peer).start()
    for half in range(2):
        kv_own(half).start()
    for peer in peers(nz, c):
        q_one(0, peer).start()
    q_own(0).start()

    lane = iota((1, 128), 1)
    plan = route_ref[pl.ds(pl.multiple_of(g * z.lanes, z.lanes), z.lanes), :]
    upper = (iota((128, 128), 0) < iota((128, 128), 1)).astype(F32).astype(BF16)
    running = jnp.zeros((nd, 1), F32)
    for i in range(z.lanes):
        mine = (plan[i : i + 1, :] == iota((nd, 128), 0)).astype(F32)
        before = jnp.dot(mine.astype(BF16), upper, preferred_element_type=F32) + running
        rank = jnp.sum(mine * before, axis=0, keepdims=True)
        target[i : i + 1, :] = plan[i : i + 1, :] * z.cap + rank.astype(I32)
        running = running + jnp.sum(mine, axis=1, keepdims=True)

    def pick_batch(j, _):
        first = j * (BATCH * z.cap)
        rows = iota((BATCH * z.cap, 128), 0) + first
        for i in range(z.lanes):
            hit = rows == target[i : i + 1, :]
            pick[j, :, i * 128 : (i + 1) * 128] = jnp.where(hit, 1.0, 0.0).astype(BF16)
        return 0

    lax.fori_loop(0, z.batches, pick_batch, 0)

    arriving = (route_ref[...] == g).astype(F32)
    tally = jnp.sum(arriving.reshape(nd, z.lanes, 128), axis=1)
    count = jnp.sum(tally, axis=1, keepdims=True)
    lower = (iota((nd, nd), 1) < iota((nd, nd), 0)).astype(F32).astype(BF16)
    start = jnp.sum(
        jnp.dot(lower, tally.astype(BF16), preferred_element_type=F32), axis=1, keepdims=True
    )
    live_col[...] = jnp.broadcast_to(jnp.sum(count, axis=0, keepdims=True), (8, 128)).astype(I32)
    count, start = count.astype(I32), start.astype(I32)
    for i in range(z.tiles):
        offset = iota((nd, 128), 1) + i * 128 - z.cap * iota((nd, 128), 0)
        held = (offset >= 0) & (offset < z.cap) & (offset < count)
        slot = jnp.sum(jnp.where(held, (start + offset + 1).astype(F32), 0.0), axis=0, keepdims=True)
        pos[i : i + 1, :] = slot.astype(I32) - 1

    per = z.block // 128

    def tri(b, k):
        return b * z.blocks - (b * (b - 1)) // 2 + (k - b)

    def place_row(b, _):
        rows = iota((z.block, 128), 0) + b * z.block

        def place_one(k, _):
            for i in range(per):
                hit = rows == pos[pl.ds(k * per + i, 1), :]
                place[tri(b, k), :, i * 128 : (i + 1) * 128] = jnp.where(hit, 1.0, 0.0).astype(BF16)
            return 0

        return lax.fori_loop(b, z.blocks, place_one, 0)

    lax.fori_loop(0, z.blocks, place_row, 0)

    lead = z.doc_most // 128
    key_doc[0:lead, :] = jnp.full((lead, 128), -1, I32)
    key_doc[lead : lead + z.tiles, :] = doc_ref[...]
    for i in range(z.tiles):
        row = jnp.broadcast_to(doc_ref[i : i + 1, :].astype(F32), (128, 128))
        query_doc[i * 128 : (i + 1) * 128, :] = row.T.astype(I32)
    pkv[0 : z.doc_most, :] = jnp.zeros((z.doc_most, 2 * hd), BF16)

    for half in range(2):
        kv_own(half).wait()
    for peer in peers(nz, c):
        for half in range(2):
            kv_one_in(half, peer).wait_recv()

    def kv_two(k):
        other = lax.rem(quarter + k, z.team)
        block = kvg.at[:, quarter]
        return remote(block, block, k2_s.at[k], k2_r.at[k], "ctx", quad + other)

    def kv_two_in(k):
        other = lax.rem(quarter - k + z.team, z.team)
        block = kvg.at[:, other]
        return remote(block, block, k2_s.at[k], k2_r.at[k], "ctx", quad + other)

    for k in range(1, z.team):
        kv_two(k).start()
    for e in range(1, z.local):
        for peer in peers(nz, c):
            q_one(e, peer).start()
        q_own(e).start()
    for k in range(1, z.team):
        kv_two_in(k).wait_recv()

    def exchange(rows, send, recv, send_sem, recv_sem, own_sem):
        first = g // BATCH

        def rows_of(ref, s):
            return ref.at[pl.ds(pl.multiple_of(s * z.cap, z.cap), z.cap)]

        def leave(s):
            return remote(rows_of(send, s), rows_of(recv, g), send_sem.at[s], recv_sem.at[g], "dp", s)

        def stay():
            return pltpu.make_async_copy(rows_of(send, g), rows_of(recv, g), own_sem)

        def body(j, _):
            j = lax.rem(first + j, z.batches)
            block = jnp.dot(pick[j], rows, preferred_element_type=F32).astype(BF16)
            height = BATCH * z.cap
            send[pl.ds(pl.multiple_of(j * height, height), height), :] = block
            for i in range(BATCH):
                s = j * BATCH + i

                @pl.when(s != g)
                def _():
                    leave(s).start()

                @pl.when(s == g)
                def _():
                    stay().start()

            return 0

        lax.fori_loop(0, z.batches, body, 0)

        def arrive():
            def body(k, _):
                s = lax.rem(g + k, nd)
                block = rows_of(recv, s)
                remote(block, block, send_sem.at[s], recv_sem.at[s], "dp", s).wait_recv()
                return 0

            stay().wait()
            lax.fori_loop(1, nd, body, 0)

        def finish():
            def body(k, _):
                leave(lax.rem(g + k, nd)).wait_send()
                return 0

            lax.fori_loop(1, nd, body, 0)

        return arrive, finish

    def compact(recv, dst, base, width):
        def body(b, _):
            def inner(k, acc):
                part = recv[pl.ds(pl.multiple_of(k * z.block, z.block), z.block), :]
                return acc + jnp.dot(place[tri(b, k)], part, preferred_element_type=F32)

            acc = lax.fori_loop(b, z.blocks, inner, jnp.zeros((z.block, width), F32))
            dst[pl.ds(pl.multiple_of(base + b * z.block, z.block), z.block), :] = acc.astype(BF16)
            return 0

        lax.fori_loop(0, z.blocks, body, 0)

    factor = float(hd**-0.5 * 1.4426950408889634)
    wide = z.window // 128

    def attend(e):
        def body(b, _):
            at = pl.multiple_of(b * z.block, z.block)
            queries = pq[pl.ds(at, z.block), :]
            keys = pkv[pl.ds(at, z.window), 0:hd]
            scores = lax.dot_general(
                queries, keys, (((1,), (1,)), ((), ())), preferred_element_type=F32
            )
            own_doc = query_doc[pl.ds(at, z.block), :]
            cuts = []
            for i in range(wide):
                ok = own_doc == key_doc[pl.ds(b * per + i, 1), :]
                j = i - (wide - per)
                if j >= 0:
                    ok = ok & (iota((z.block, 128), 1) + j * 128 <= iota((z.block, 128), 0))
                cuts.append(jnp.where(ok, scores[:, i * 128 : (i + 1) * 128], NEG))
            masked = jnp.concatenate(cuts, axis=1)
            top = jnp.max(masked, axis=1, keepdims=True)
            exponent = jnp.exp2((masked - top) * factor)
            total = jnp.sum(exponent, axis=1, keepdims=True)
            values = pkv[pl.ds(at, z.window), hd : 2 * hd]
            mixed = jnp.dot(exponent.astype(BF16), values, preferred_element_type=F32) / total
            alive = iota((z.block, hd), 0) + at < live_col[0:1, :]
            ob[e, pl.ds(at, z.block), :] = jnp.where(alive, mixed, 0.0).astype(BF16)
            return 0

        lax.fori_loop(0, z.blocks, body, 0)

    def out_cols(peer, e):
        return pl.ds(pl.multiple_of((peer * z.local + e) * hd, hd), hd)

    def out_rows(peer, e):
        return ob.at[e, pl.ds(pl.multiple_of(peer * z.slots, z.slots), z.slots)]

    def o_one(e, peer):
        dst = out_ref.at[:, out_cols(c, e)]
        return remote(out_rows(peer, e), dst, o_s.at[e, peer], o_r.at[e, c], "ctx", peer)

    def o_one_in(e, peer):
        dst = out_ref.at[:, out_cols(peer, e)]
        return remote(out_rows(peer, e), dst, o_s.at[e, peer], o_r.at[e, peer], "ctx", peer)

    def o_own(e):
        return pltpu.make_async_copy(
            out_rows(c, e), out_ref.at[:, out_cols(c, e)], own.at[2 + z.local + e]
        )

    kv_rows = kvg[...].reshape(z.group, 2 * hd)
    kv_arrive, kv_finish = exchange(
        kv_rows, send_kv, recv_kv, dkv_s, dkv_r, own.at[2 + 2 * z.local]
    )
    finishes = [kv_finish]
    for e in range(z.local):
        q_own(e).wait()
        for peer in peers(nz, c):
            q_one_in(e, peer).wait_recv()
        q_arrive, q_finish = exchange(
            qg[e].reshape(z.group, hd), send_q.at[e], recv_q.at[e], dq_s.at[e], dq_r.at[e],
            own.at[3 + 2 * z.local + e],
        )
        finishes.append(q_finish)
        if e == 0:
            kv_arrive()
            compact(recv_kv, pkv, z.doc_most, 2 * hd)
        q_arrive()
        compact(recv_q.at[e], pq, 0, hd)
        attend(e)
        for peer in peers(nz, c):
            o_one(e, peer).start()
        o_own(e).start()

    for peer in peers(nz, c):
        for half in range(2):
            kv_one(half, peer).wait_send()
        for e in range(z.local):
            q_one(e, peer).wait_send()
    for k in range(1, z.team):
        kv_two(k).wait_send()
    for finish in finishes:
        finish()
    for e in range(z.local):
        o_own(e).wait()
        for peer in peers(nz, c):
            o_one_in(e, peer).wait_recv()
        for peer in peers(nz, c):
            o_one(e, peer).wait_send()


def call(z, route, docs, q_src, kv_src):
    hd = HEAD_DIM
    dma = pltpu.SemaphoreType.DMA
    vmem = pltpu.VMEM
    tri_blocks = z.blocks * (z.blocks + 1) // 2
    return pl.pallas_call(
        functools.partial(kernel, z),
        out_shape=jax.ShapeDtypeStruct((z.slots, z.heads * hd), BF16),
        in_specs=[
            pl.BlockSpec(memory_space=pltpu.VMEM),
            pl.BlockSpec(memory_space=pltpu.VMEM),
            pl.BlockSpec(memory_space=pl.ANY),
            pl.BlockSpec(memory_space=pl.ANY),
        ],
        out_specs=pl.BlockSpec(memory_space=pl.ANY),
        scratch_shapes=[
            vmem((z.local, z.ctx, z.rows, hd), BF16),
            vmem((z.ctx, z.team, z.part, 2 * hd), BF16),
            vmem((z.local, z.pack, hd), BF16),
            vmem((z.pack, 2 * hd), BF16),
            vmem((z.local, z.pack, hd), BF16),
            vmem((z.pack, 2 * hd), BF16),
            vmem((z.pack, hd), BF16),
            vmem((z.doc_most + z.pack, 2 * hd), BF16),
            vmem((z.local, z.pack, hd), BF16),
            vmem((z.batches, BATCH * z.cap, z.group), BF16),
            vmem((tri_blocks, z.block, z.block), BF16),
            vmem((z.lanes, 128), I32),
            vmem((z.tiles, 128), I32),
            vmem((z.doc_most // 128 + z.tiles, 128), I32),
            vmem((z.pack, 128), I32),
            vmem((8, 128), I32),
            dma((z.local, z.ctx)),
            dma((z.local, z.ctx)),
            dma((2, z.ctx)),
            dma((2, z.ctx)),
            dma((z.team,)),
            dma((z.team,)),
            dma((z.dp,)),
            dma((z.dp,)),
            dma((z.local, z.dp)),
            dma((z.local, z.dp)),
            dma((z.local, z.ctx)),
            dma((z.local, z.ctx)),
            dma((3 + 3 * z.local,)),
        ],
        compiler_params=pltpu.CompilerParams(
            collective_id=0, has_side_effects=True, vmem_limit_bytes=56 << 20
        ),
    )(route, docs, q_src, kv_src)


def on_device(z, q_src, kv_src, route, doc_ids):
    return call(z, route.reshape(-1, 128), doc_ids.reshape(-1, 128), q_src, kv_src)


def solution(mesh):
    z = Sizes(
        mesh.shape["dp"], mesh.shape["ctx"], 128, 96, Q_HEADS, KV_HEADS, DOC_MOST, BLOCK
    )
    in_specs = (P(("dp", "ctx"), None), P(("dp", "ctx"), None), P(), P("dp", None))
    return jax.shard_map(
        functools.partial(on_device, z),
        mesh=mesh,
        in_specs=in_specs,
        out_specs=P(("dp", "ctx"), None),
        check_vma=False,
    )
```

```python
import functools
import math

import jax
import jax.numpy as jnp
from jax import lax
from jax.experimental import pallas as pl
from jax.experimental.pallas import tpu as pltpu
from jax.sharding import PartitionSpec as P

Q_HEADS = 32
KV_HEADS = 4
HEAD_DIM = 128
DOC_MOST = 1024
BLOCK = 256
BATCH = 4
NEG = -1e30
MESH = pl.DeviceIdType.MESH
BF16 = jnp.bfloat16
F32 = jnp.float32
I32 = jnp.int32


class Sizes:
    def __init__(self, dp, ctx, rows, cap, heads, kv_heads, doc_most, block):
        self.dp, self.ctx, self.rows, self.cap = dp, ctx, rows, cap
        self.heads, self.kv_heads = heads, kv_heads
        self.local = heads // ctx
        self.team = ctx // kv_heads
        self.group = rows * ctx
        self.pack = dp * cap
        self.slots = self.pack // ctx
        self.part = rows // self.team
        self.lanes = self.group // 128
        self.tiles = self.pack // 128
        self.doc_most, self.block = doc_most, block
        self.blocks = self.pack // block
        self.window = doc_most + block
        self.batches = dp // BATCH
        self.span = math.gcd(self.pack, 2 * block)
        self.pieces = math.gcd(self.blocks, 4)


def iota(shape, dim):
    return lax.broadcasted_iota(I32, shape, dim)


def alternating(n):
    order = []
    for k in range(1, n // 2):
        order += [k, n - k]
    return order + [n // 2]


def kernel(
    z, route_ref, doc_ref, q_hbm, kv_hbm, out_ref,
    qg, kvg, send_q, send_kv, recv_q, recv_kv, pq, pkv, ob, pick, place,
    target, pos, key_doc, query_doc, live_col,
    zq_s, zq_r, k1_s, k1_r, k2_s, k2_r, dkv_s, dkv_r, dq_s, dq_r, o_s, o_r, own,
):
    g = lax.axis_index("dp")
    c = lax.axis_index("ctx")
    nz, nd, hd = z.ctx, z.dp, HEAD_DIM
    quarter = lax.rem(c, z.team)
    quad = c - quarter

    barrier = pltpu.get_barrier_semaphore()

    def greet(axis, me, n):
        def body(k, _):
            pl.semaphore_signal(
                barrier, inc=1, device_id={axis: lax.rem(me + k, n)}, device_id_type=MESH
            )
            return 0

        lax.fori_loop(1, n, body, 0)

    greet("ctx", c, nz)
    greet("dp", g, nd)
    pl.semaphore_wait(barrier, nz + nd - 2)

    def remote(src, dst, s, r, axis, peer):
        return pltpu.make_async_remote_copy(
            src_ref=src, dst_ref=dst, send_sem=s, recv_sem=r,
            device_id={axis: peer}, device_id_type=MESH,
        )

    def kv_cut(half, peer):
        part = lax.rem(peer, z.team)
        head = peer // z.team
        rows = pl.ds(pl.multiple_of(part * z.part, z.part), z.part)
        cols = pl.ds(pl.multiple_of((half * z.kv_heads + head) * hd, hd), hd)
        return kv_hbm.at[rows, cols], part

    def kv_one(half, peer):
        src, part = kv_cut(half, peer)
        dst = kvg.at[c, part, :, pl.ds(half * hd, hd)]
        return remote(src, dst, k1_s.at[half, peer], k1_r.at[half, c], "ctx", peer)

    def kv_one_in(half, peer):
        dst = kvg.at[peer, quarter, :, pl.ds(half * hd, hd)]
        return remote(dst, dst, k1_s.at[half, peer], k1_r.at[half, peer], "ctx", peer)

    def kv_own(half):
        src, part = kv_cut(half, c)
        return pltpu.make_async_copy(
            src, kvg.at[c, part, :, pl.ds(half * hd, hd)], own.at[half]
        )

    def q_cut(e, peer):
        return q_hbm.at[:, pl.ds(pl.multiple_of((peer * z.local + e) * hd, hd), hd)]

    def q_one(e, peer):
        return remote(q_cut(e, peer), qg.at[e, c], zq_s.at[e, peer], zq_r.at[e, c], "ctx", peer)

    def q_one_in(e, peer):
        dst = qg.at[e, peer]
        return remote(dst, dst, zq_s.at[e, peer], zq_r.at[e, peer], "ctx", peer)

    def q_own(e):
        return pltpu.make_async_copy(q_cut(e, c), qg.at[e, c], own.at[2 + e])

    def peers(n, me):
        return [lax.rem(me + k, n) for k in alternating(n)]

    for peer in peers(nz, c):
        for half in range(2):
            kv_one(half, peer).start()
    for half in range(2):
        kv_own(half).start()
    for peer in peers(nz, c):
        q_one(0, peer).start()
    q_own(0).start()

    lane = iota((1, 128), 1)
    plan = route_ref[pl.ds(pl.multiple_of(g * z.lanes, z.lanes), z.lanes), :]
    upper = (iota((128, 128), 0) < iota((128, 128), 1)).astype(F32).astype(BF16)
    running = jnp.zeros((nd, 1), F32)
    for i in range(z.lanes):
        mine = (plan[i : i + 1, :] == iota((nd, 128), 0)).astype(F32)
        before = jnp.dot(mine.astype(BF16), upper, preferred_element_type=F32) + running
        rank = jnp.sum(mine * before, axis=0, keepdims=True)
        target[i : i + 1, :] = plan[i : i + 1, :] * z.cap + rank.astype(I32)
        running = running + jnp.sum(mine, axis=1, keepdims=True)

    def pick_batch(j, _):
        first = j * (BATCH * z.cap)
        rows = iota((BATCH * z.cap, 128), 0) + first
        for i in range(z.lanes):
            hit = rows == target[i : i + 1, :]
            pick[j, :, i * 128 : (i + 1) * 128] = jnp.where(hit, 1.0, 0.0).astype(BF16)
        return 0

    lax.fori_loop(0, z.batches, pick_batch, 0)

    for half in range(2):
        kv_own(half).wait()
    for peer in peers(nz, c):
        for half in range(2):
            kv_one_in(half, peer).wait_recv()

    def kv_two(k):
        other = lax.rem(quarter + k, z.team)
        block = kvg.at[:, quarter]
        return remote(block, block, k2_s.at[k], k2_r.at[k], "ctx", quad + other)

    def kv_two_in(k):
        other = lax.rem(quarter - k + z.team, z.team)
        block = kvg.at[:, other]
        return remote(block, block, k2_s.at[k], k2_r.at[k], "ctx", quad + other)

    for k in range(1, z.team):
        kv_two(k).start()
    for e in range(1, z.local):
        for peer in peers(nz, c):
            q_one(e, peer).start()
        q_own(e).start()
    arriving = (route_ref[...] == g).astype(F32)
    tally = jnp.sum(arriving.reshape(nd, z.lanes, 128), axis=1)
    count = jnp.sum(tally, axis=1, keepdims=True)
    lower = (iota((nd, nd), 1) < iota((nd, nd), 0)).astype(F32).astype(BF16)
    start = jnp.sum(
        jnp.dot(lower, tally.astype(BF16), preferred_element_type=F32), axis=1, keepdims=True
    )
    live_col[...] = jnp.broadcast_to(jnp.sum(count, axis=0, keepdims=True), (8, 128)).astype(I32)
    count, start = count.astype(I32), start.astype(I32)
    for i in range(z.tiles):
        offset = iota((nd, 128), 1) + i * 128 - z.cap * iota((nd, 128), 0)
        held = (offset >= 0) & (offset < z.cap) & (offset < count)
        slot = jnp.sum(jnp.where(held, (start + offset + 1).astype(F32), 0.0), axis=0, keepdims=True)
        pos[i : i + 1, :] = slot.astype(I32) - 1

    per = z.block // 128

    def place_row(b, _):
        rows = iota((z.span, 128), 0) + b * z.span

        def place_one(k, _):
            hit = rows == pos[pl.ds(k, 1), :]
            cols = pl.ds(pl.multiple_of(k * 128, 128), 128)
            place[pl.ds(pl.multiple_of(b * z.span, z.span), z.span), cols] = jnp.where(
                hit, 1.0, 0.0
            ).astype(BF16)
            return 0

        return lax.fori_loop(b * (z.span // 128), z.tiles, place_one, 0)

    lax.fori_loop(0, z.pack // z.span, place_row, 0)

    lead = z.doc_most // 128
    key_doc[0:lead, :] = jnp.full((lead, 128), -1, I32)
    key_doc[lead : lead + z.tiles, :] = doc_ref[...]
    for i in range(z.tiles):
        row = jnp.broadcast_to(doc_ref[i : i + 1, :].astype(F32), (128, 128))
        query_doc[i * 128 : (i + 1) * 128, :] = row.T.astype(I32)
    pkv[0 : z.doc_most, :] = jnp.zeros((z.doc_most, 2 * hd), BF16)

    for k in range(1, z.team):
        kv_two_in(k).wait_recv()

    def exchange(rows, send, recv, send_sem, recv_sem, own_sem):
        first = g // BATCH

        def rows_of(ref, s):
            return ref.at[pl.ds(pl.multiple_of(s * z.cap, z.cap), z.cap)]

        def leave(s):
            return remote(rows_of(send, s), rows_of(recv, g), send_sem.at[s], recv_sem.at[g], "dp", s)

        def stay():
            return pltpu.make_async_copy(rows_of(send, g), rows_of(recv, g), own_sem)

        def body(j, _):
            j = lax.rem(first + j, z.batches)
            block = jnp.dot(pick[j], rows, preferred_element_type=F32).astype(BF16)
            height = BATCH * z.cap
            send[pl.ds(pl.multiple_of(j * height, height), height), :] = block
            for i in range(BATCH):
                s = j * BATCH + i

                @pl.when(s != g)
                def _():
                    leave(s).start()

                @pl.when(s == g)
                def _():
                    stay().start()

            return 0

        lax.fori_loop(0, z.batches, body, 0)

        def arrive():
            def body(k, _):
                s = lax.rem(g + k, nd)
                block = rows_of(recv, s)
                remote(block, block, send_sem.at[s], recv_sem.at[s], "dp", s).wait_recv()
                return 0

            stay().wait()
            lax.fori_loop(1, nd, body, 0)

        def finish():
            def body(k, _):
                leave(lax.rem(g + k, nd)).wait_send()
                return 0

            lax.fori_loop(1, nd, body, 0)

        return arrive, finish

    def compact(recv, dst, base):
        for b in range(0, z.pack, z.span):
            rows = jnp.dot(
                place[b : b + z.span, b : z.pack], recv[b : z.pack, :], preferred_element_type=F32
            )
            dst[base + b : base + b + z.span, :] = rows.astype(BF16)

    factor = float(hd**-0.5 * 1.4426950408889634)
    wide = z.window // 128

    def attend(e, first, count):
        def body(b, _):
            at = pl.multiple_of(b * z.block, z.block)
            queries = pq[pl.ds(at, z.block), :]
            keys = pkv[pl.ds(at, z.window), 0:hd]
            scores = lax.dot_general(
                queries, keys, (((1,), (1,)), ((), ())), preferred_element_type=F32
            )
            own_doc = query_doc[pl.ds(at, z.block), :]
            cuts = []
            for i in range(wide):
                ok = own_doc == key_doc[pl.ds(b * per + i, 1), :]
                j = i - (wide - per)
                if j >= 0:
                    ok = ok & (iota((z.block, 128), 1) + j * 128 <= iota((z.block, 128), 0))
                cuts.append(jnp.where(ok, scores[:, i * 128 : (i + 1) * 128], NEG))
            masked = jnp.concatenate(cuts, axis=1)
            top = jnp.max(masked, axis=1, keepdims=True)
            exponent = jnp.exp2((masked - top) * factor)
            total = jnp.sum(exponent, axis=1, keepdims=True)
            values = pkv[pl.ds(at, z.window), hd : 2 * hd]
            mixed = jnp.dot(exponent.astype(BF16), values, preferred_element_type=F32) / total
            alive = iota((z.block, hd), 0) + at < live_col[0:1, :]
            ob[e, pl.ds(at, z.block), :] = jnp.where(alive, mixed, 0.0).astype(BF16)
            return 0

        lax.fori_loop(first, first + count, body, 0)

    def out_cols(peer, e):
        return pl.ds(pl.multiple_of((peer * z.local + e) * hd, hd), hd)

    def out_rows(peer, e):
        return ob.at[e, pl.ds(pl.multiple_of(peer * z.slots, z.slots), z.slots)]

    def o_one(e, peer):
        dst = out_ref.at[:, out_cols(c, e)]
        return remote(out_rows(peer, e), dst, o_s.at[e, peer], o_r.at[e, c], "ctx", peer)

    def o_one_in(e, peer):
        dst = out_ref.at[:, out_cols(peer, e)]
        return remote(out_rows(peer, e), dst, o_s.at[e, peer], o_r.at[e, peer], "ctx", peer)

    def o_own(e):
        return pltpu.make_async_copy(
            out_rows(c, e), out_ref.at[:, out_cols(c, e)], own.at[2 + z.local + e]
        )

    kv_rows = kvg[...].reshape(z.group, 2 * hd)
    kv_arrive, kv_finish = exchange(
        kv_rows, send_kv, recv_kv, dkv_s, dkv_r, own.at[2 + 2 * z.local]
    )
    finishes = [kv_finish]
    for e in range(z.local):
        q_own(e).wait()
        for peer in peers(nz, c):
            q_one_in(e, peer).wait_recv()
        q_arrive, q_finish = exchange(
            qg[e].reshape(z.group, hd), send_q.at[e], recv_q.at[e], dq_s.at[e], dq_r.at[e],
            own.at[3 + 2 * z.local + e],
        )
        finishes.append(q_finish)
        if e == 0:
            kv_arrive()
            compact(recv_kv, pkv, z.doc_most)
        q_arrive()
        compact(recv_q.at[e], pq, 0)
        run, owners = z.blocks // z.pieces, nz // z.pieces
        home, way = c // owners, 1 + (z.pieces - 2) * lax.rem(c, 2)
        for turn in range(z.pieces):
            step = (way, z.pieces // 2, z.pieces - way, 0)[turn] if z.pieces == 4 else turn
            piece = lax.rem(home + step, z.pieces)
            attend(e, piece * run, run)
            for i in range(owners):
                peer = piece * owners + i

                @pl.when(peer != c)
                def _():
                    o_one(e, peer).start()

                @pl.when(peer == c)
                def _():
                    o_own(e).start()

    for peer in peers(nz, c):
        for half in range(2):
            kv_one(half, peer).wait_send()
        for e in range(z.local):
            q_one(e, peer).wait_send()
    for k in range(1, z.team):
        kv_two(k).wait_send()
    for finish in finishes:
        finish()
    for e in range(z.local):
        o_own(e).wait()
        for peer in peers(nz, c):
            o_one_in(e, peer).wait_recv()
        for peer in peers(nz, c):
            o_one(e, peer).wait_send()


def call(z, route, docs, q_src, kv_src):
    hd = HEAD_DIM
    dma = pltpu.SemaphoreType.DMA
    vmem = pltpu.VMEM
    return pl.pallas_call(
        functools.partial(kernel, z),
        out_shape=jax.ShapeDtypeStruct((z.slots, z.heads * hd), BF16),
        in_specs=[
            pl.BlockSpec(memory_space=pltpu.VMEM),
            pl.BlockSpec(memory_space=pltpu.VMEM),
            pl.BlockSpec(memory_space=pl.ANY),
            pl.BlockSpec(memory_space=pl.ANY),
        ],
        out_specs=pl.BlockSpec(memory_space=pl.ANY),
        scratch_shapes=[
            vmem((z.local, z.ctx, z.rows, hd), BF16),
            vmem((z.ctx, z.team, z.part, 2 * hd), BF16),
            vmem((z.local, z.pack, hd), BF16),
            vmem((z.pack, 2 * hd), BF16),
            vmem((z.local, z.pack, hd), BF16),
            vmem((z.pack, 2 * hd), BF16),
            vmem((z.pack, hd), BF16),
            vmem((z.doc_most + z.pack, 2 * hd), BF16),
            vmem((z.local, z.pack, hd), BF16),
            vmem((z.batches, BATCH * z.cap, z.group), BF16),
            vmem((z.pack, z.pack), BF16),
            vmem((z.lanes, 128), I32),
            vmem((z.tiles, 128), I32),
            vmem((z.doc_most // 128 + z.tiles, 128), I32),
            vmem((z.pack, 128), I32),
            vmem((8, 128), I32),
            dma((z.local, z.ctx)),
            dma((z.local, z.ctx)),
            dma((2, z.ctx)),
            dma((2, z.ctx)),
            dma((z.team,)),
            dma((z.team,)),
            dma((z.dp,)),
            dma((z.dp,)),
            dma((z.local, z.dp)),
            dma((z.local, z.dp)),
            dma((z.local, z.ctx)),
            dma((z.local, z.ctx)),
            dma((3 + 3 * z.local,)),
        ],
        compiler_params=pltpu.CompilerParams(
            collective_id=0, has_side_effects=True, vmem_limit_bytes=56 << 20
        ),
    )(route, docs, q_src, kv_src)


def on_device(z, q_src, kv_src, route, doc_ids):
    return call(z, route.reshape(-1, 128), doc_ids.reshape(-1, 128), q_src, kv_src)


def solution(mesh):
    z = Sizes(
        mesh.shape["dp"], mesh.shape["ctx"], 128, 96, Q_HEADS, KV_HEADS, DOC_MOST, BLOCK
    )
    in_specs = (P(("dp", "ctx"), None), P(("dp", "ctx"), None), P(), P("dp", None))
    return jax.shard_map(
        functools.partial(on_device, z),
        mesh=mesh,
        in_specs=in_specs,
        out_specs=P(("dp", "ctx"), None),
        check_vma=False,
    )
```

```python
import functools
import math

import jax
import jax.numpy as jnp
from jax import lax
from jax.experimental import pallas as pl
from jax.experimental.pallas import tpu as pltpu
from jax.sharding import PartitionSpec as P

Q_HEADS = 32
KV_HEADS = 4
HEAD_DIM = 128
DOC_MOST = 1024
BLOCK = 256
BATCH = 4
NEG = -1e30
MESH = pl.DeviceIdType.MESH
BF16 = jnp.bfloat16
F32 = jnp.float32
I32 = jnp.int32


class Sizes:
    def __init__(self, dp, ctx, rows, cap, heads, kv_heads, doc_most, block):
        self.dp, self.ctx, self.rows, self.cap = dp, ctx, rows, cap
        self.heads, self.kv_heads = heads, kv_heads
        self.local = heads // ctx
        self.team = ctx // kv_heads
        self.group = rows * ctx
        self.pack = dp * cap
        self.slots = self.pack // ctx
        self.part = rows // self.team
        self.lanes = self.group // 128
        self.tiles = self.pack // 128
        self.doc_most, self.block = doc_most, block
        self.blocks = self.pack // block
        self.window = doc_most + block
        self.batches = dp // BATCH
        self.span = math.gcd(self.pack, 2 * block)
        self.pieces = math.gcd(self.blocks, 4)


def iota(shape, dim):
    return lax.broadcasted_iota(I32, shape, dim)


def alternating(n):
    order = []
    for k in range(n // 2 - 1, 0, -1):
        order += [k, n - k]
    return order


def kernel(
    z, route_ref, doc_ref, q_hbm, kv_hbm, out_ref,
    qg, kvg, send_q, send_kv, recv_q, recv_kv, pq, pkv, ob, pick, place,
    target, pos, key_doc, query_doc, live_col, relay_q, relay_o,
    hop_s, hop_r, end_s, end_r, zq_s, zq_r, k1_s, k1_r, k2_s, k2_r, dkv_s, dkv_r, dq_s, dq_r, o_s, o_r, own,
):
    g = lax.axis_index("dp")
    c = lax.axis_index("ctx")
    nz, nd, hd = z.ctx, z.dp, HEAD_DIM
    quarter = lax.rem(c, z.team)
    quad = c - quarter

    barrier = pltpu.get_barrier_semaphore()

    def greet(axis, me, n):
        def body(k, _):
            pl.semaphore_signal(
                barrier, inc=1, device_id={axis: lax.rem(me + k, n)}, device_id_type=MESH
            )
            return 0

        lax.fori_loop(1, n, body, 0)

    greet("ctx", c, nz)
    greet("dp", g, nd)
    pl.semaphore_wait(barrier, nz + nd - 2)

    def remote(src, dst, s, r, axis, peer):
        return pltpu.make_async_remote_copy(
            src_ref=src, dst_ref=dst, send_sem=s, recv_sem=r,
            device_id={axis: peer}, device_id_type=MESH,
        )

    def kv_cut(half, peer):
        part = lax.rem(peer, z.team)
        head = peer // z.team
        rows = pl.ds(pl.multiple_of(part * z.part, z.part), z.part)
        cols = pl.ds(pl.multiple_of((half * z.kv_heads + head) * hd, hd), hd)
        return kv_hbm.at[rows, cols], part

    def kv_one(half, peer):
        src, part = kv_cut(half, peer)
        dst = kvg.at[c, part, :, pl.ds(half * hd, hd)]
        return remote(src, dst, k1_s.at[half, peer], k1_r.at[half, c], "ctx", peer)

    def kv_one_in(half, peer):
        dst = kvg.at[peer, quarter, :, pl.ds(half * hd, hd)]
        return remote(dst, dst, k1_s.at[half, peer], k1_r.at[half, peer], "ctx", peer)

    def kv_own(half):
        src, part = kv_cut(half, c)
        return pltpu.make_async_copy(
            src, kvg.at[c, part, :, pl.ds(half * hd, hd)], own.at[half]
        )

    def q_cut(e, peer):
        return q_hbm.at[:, pl.ds(pl.multiple_of((peer * z.local + e) * hd, hd), hd)]

    def q_one(e, peer):
        return remote(q_cut(e, peer), qg.at[e, c], zq_s.at[e, peer], zq_r.at[e, c], "ctx", peer)

    def q_one_in(e, peer):
        dst = qg.at[e, peer]
        return remote(dst, dst, zq_s.at[e, peer], zq_r.at[e, peer], "ctx", peer)

    def q_own(e):
        return pltpu.make_async_copy(q_cut(e, c), qg.at[e, c], own.at[2 + e])

    def peers(n, me):
        return [lax.rem(me + k, n) for k in alternating(n)]

    facing = lax.rem(c + nz // 2, nz)
    turns = (nz // 4, nz - nz // 4)

    def half_of(ref, way, n):
        return ref.at[pl.ds(way * (n // 2), n // 2)]

    def hop(block, relay, kind, e, way):
        peer = lax.rem(c + turns[way], nz)
        return remote(
            block, relay.at[e, way], hop_s.at[kind, e, way], hop_r.at[kind, e, way], "ctx", peer
        )

    def hand_on(relay, dst, kind, e, way):
        peer = lax.rem(c + turns[way], nz)
        return remote(
            relay.at[e, way], dst, end_s.at[kind, e, way], end_r.at[kind, e, way], "ctx", peer
        )

    def q_hop(e, way):
        return hop(half_of(q_cut(e, facing), way, z.rows), relay_q, 0, e, way)

    def q_pass(e, way):
        origin = lax.rem(c + turns[1 - way], nz)
        return hand_on(relay_q, half_of(qg.at[e, origin], way, z.rows), 0, e, way)

    def q_end(e, way):
        return hand_on(relay_q, half_of(qg.at[e, facing], way, z.rows), 0, e, way)

    def send_q_rows(e):
        for way in range(2):
            q_hop(e, way).start()
        for peer in peers(nz, c):
            q_one(e, peer).start()
        q_own(e).start()

    def pass_q_rows(e):
        for way in range(2):
            q_hop(e, way).wait_recv()
            q_pass(e, way).start()

    for peer in peers(nz, c) + [facing]:
        for half in range(2):
            kv_one(half, peer).start()
    for half in range(2):
        kv_own(half).start()
    send_q_rows(0)

    lane = iota((1, 128), 1)
    plan = route_ref[pl.ds(pl.multiple_of(g * z.lanes, z.lanes), z.lanes), :]
    upper = (iota((128, 128), 0) < iota((128, 128), 1)).astype(F32).astype(BF16)
    running = jnp.zeros((nd, 1), F32)
    for i in range(z.lanes):
        mine = (plan[i : i + 1, :] == iota((nd, 128), 0)).astype(F32)
        before = jnp.dot(mine.astype(BF16), upper, preferred_element_type=F32) + running
        rank = jnp.sum(mine * before, axis=0, keepdims=True)
        target[i : i + 1, :] = plan[i : i + 1, :] * z.cap + rank.astype(I32)
        running = running + jnp.sum(mine, axis=1, keepdims=True)

    def pick_batch(j, _):
        first = j * (BATCH * z.cap)
        rows = iota((BATCH * z.cap, 128), 0) + first
        for i in range(z.lanes):
            hit = rows == target[i : i + 1, :]
            pick[j, :, i * 128 : (i + 1) * 128] = jnp.where(hit, 1.0, 0.0).astype(BF16)
        return 0

    lax.fori_loop(0, z.batches, pick_batch, 0)

    for half in range(2):
        kv_own(half).wait()
    for peer in peers(nz, c) + [facing]:
        for half in range(2):
            kv_one_in(half, peer).wait_recv()

    def kv_two(k):
        other = lax.rem(quarter + k, z.team)
        block = kvg.at[:, quarter]
        return remote(block, block, k2_s.at[k], k2_r.at[k], "ctx", quad + other)

    def kv_two_in(k):
        other = lax.rem(quarter - k + z.team, z.team)
        block = kvg.at[:, other]
        return remote(block, block, k2_s.at[k], k2_r.at[k], "ctx", quad + other)

    for k in range(1, z.team):
        kv_two(k).start()
    pass_q_rows(0)
    for e in range(1, z.local):
        send_q_rows(e)
    arriving = (route_ref[...] == g).astype(F32)
    tally = jnp.sum(arriving.reshape(nd, z.lanes, 128), axis=1)
    count = jnp.sum(tally, axis=1, keepdims=True)
    lower = (iota((nd, nd), 1) < iota((nd, nd), 0)).astype(F32).astype(BF16)
    start = jnp.sum(
        jnp.dot(lower, tally.astype(BF16), preferred_element_type=F32), axis=1, keepdims=True
    )
    live_col[...] = jnp.broadcast_to(jnp.sum(count, axis=0, keepdims=True), (8, 128)).astype(I32)
    count, start = count.astype(I32), start.astype(I32)
    for i in range(z.tiles):
        offset = iota((nd, 128), 1) + i * 128 - z.cap * iota((nd, 128), 0)
        held = (offset >= 0) & (offset < z.cap) & (offset < count)
        slot = jnp.sum(jnp.where(held, (start + offset + 1).astype(F32), 0.0), axis=0, keepdims=True)
        pos[i : i + 1, :] = slot.astype(I32) - 1

    per = z.block // 128

    def place_row(b, _):
        rows = iota((z.span, 128), 0) + b * z.span

        def place_one(k, _):
            hit = rows == pos[pl.ds(k, 1), :]
            cols = pl.ds(pl.multiple_of(k * 128, 128), 128)
            place[pl.ds(pl.multiple_of(b * z.span, z.span), z.span), cols] = jnp.where(
                hit, 1.0, 0.0
            ).astype(BF16)
            return 0

        return lax.fori_loop(b * (z.span // 128), z.tiles, place_one, 0)

    lax.fori_loop(0, z.pack // z.span, place_row, 0)

    lead = z.doc_most // 128
    key_doc[0:lead, :] = jnp.full((lead, 128), -1, I32)
    key_doc[lead : lead + z.tiles, :] = doc_ref[...]
    for i in range(z.tiles):
        row = jnp.broadcast_to(doc_ref[i : i + 1, :].astype(F32), (128, 128))
        query_doc[i * 128 : (i + 1) * 128, :] = row.T.astype(I32)
    pkv[0 : z.doc_most, :] = jnp.zeros((z.doc_most, 2 * hd), BF16)

    for k in range(1, z.team):
        kv_two_in(k).wait_recv()

    def exchange(rows, send, recv, send_sem, recv_sem, own_sem):
        first = g // BATCH

        def rows_of(ref, s):
            return ref.at[pl.ds(pl.multiple_of(s * z.cap, z.cap), z.cap)]

        def leave(s):
            return remote(rows_of(send, s), rows_of(recv, g), send_sem.at[s], recv_sem.at[g], "dp", s)

        def stay():
            return pltpu.make_async_copy(rows_of(send, g), rows_of(recv, g), own_sem)

        def body(j, _):
            j = lax.rem(first + j, z.batches)
            block = jnp.dot(pick[j], rows, preferred_element_type=F32).astype(BF16)
            height = BATCH * z.cap
            send[pl.ds(pl.multiple_of(j * height, height), height), :] = block
            for i in range(BATCH):
                s = j * BATCH + i

                @pl.when(s != g)
                def _():
                    leave(s).start()

                @pl.when(s == g)
                def _():
                    stay().start()

            return 0

        lax.fori_loop(0, z.batches, body, 0)

        def arrive():
            def body(k, _):
                s = lax.rem(g + k, nd)
                block = rows_of(recv, s)
                remote(block, block, send_sem.at[s], recv_sem.at[s], "dp", s).wait_recv()
                return 0

            stay().wait()
            lax.fori_loop(1, nd, body, 0)

        def finish():
            def body(k, _):
                leave(lax.rem(g + k, nd)).wait_send()
                return 0

            lax.fori_loop(1, nd, body, 0)

        return arrive, finish

    def compact(recv, dst, base):
        for b in range(0, z.pack, z.span):
            rows = jnp.dot(
                place[b : b + z.span, b : z.pack], recv[b : z.pack, :], preferred_element_type=F32
            )
            dst[base + b : base + b + z.span, :] = rows.astype(BF16)

    factor = float(hd**-0.5 * 1.4426950408889634)
    wide = z.window // 128

    def attend(e, first, count):
        def body(b, _):
            at = pl.multiple_of(b * z.block, z.block)
            queries = pq[pl.ds(at, z.block), :]
            keys = pkv[pl.ds(at, z.window), 0:hd]
            scores = lax.dot_general(
                queries, keys, (((1,), (1,)), ((), ())), preferred_element_type=F32
            )
            own_doc = query_doc[pl.ds(at, z.block), :]
            cuts = []
            for i in range(wide):
                ok = own_doc == key_doc[pl.ds(b * per + i, 1), :]
                j = i - (wide - per)
                if j >= 0:
                    ok = ok & (iota((z.block, 128), 1) + j * 128 <= iota((z.block, 128), 0))
                cuts.append(jnp.where(ok, scores[:, i * 128 : (i + 1) * 128], NEG))
            masked = jnp.concatenate(cuts, axis=1)
            top = jnp.max(masked, axis=1, keepdims=True)
            exponent = jnp.exp2((masked - top) * factor)
            total = jnp.sum(exponent, axis=1, keepdims=True)
            values = pkv[pl.ds(at, z.window), hd : 2 * hd]
            mixed = jnp.dot(exponent.astype(BF16), values, preferred_element_type=F32) / total
            alive = iota((z.block, hd), 0) + at < live_col[0:1, :]
            ob[e, pl.ds(at, z.block), :] = jnp.where(alive, mixed, 0.0).astype(BF16)
            return 0

        lax.fori_loop(first, first + count, body, 0)

    def out_cols(peer, e):
        return pl.ds(pl.multiple_of((peer * z.local + e) * hd, hd), hd)

    def out_rows(peer, e):
        return ob.at[e, pl.ds(pl.multiple_of(peer * z.slots, z.slots), z.slots)]

    def o_one(e, peer):
        dst = out_ref.at[:, out_cols(c, e)]
        return remote(out_rows(peer, e), dst, o_s.at[e, peer], o_r.at[e, c], "ctx", peer)

    def o_one_in(e, peer):
        dst = out_ref.at[:, out_cols(peer, e)]
        return remote(out_rows(peer, e), dst, o_s.at[e, peer], o_r.at[e, peer], "ctx", peer)

    def o_own(e):
        return pltpu.make_async_copy(
            out_rows(c, e), out_ref.at[:, out_cols(c, e)], own.at[2 + z.local + e]
        )

    def o_hop(e, way):
        return hop(half_of(out_rows(facing, e), way, z.slots), relay_o, 1, e, way)

    def o_pass(e, way):
        origin = lax.rem(c + turns[1 - way], nz)
        dst = half_of(out_ref, way, z.slots).at[:, out_cols(origin, e)]
        return hand_on(relay_o, dst, 1, e, way)

    def o_end(e, way):
        dst = half_of(out_ref, way, z.slots).at[:, out_cols(facing, e)]
        return hand_on(relay_o, dst, 1, e, way)

    def pass_outputs(e):
        for way in range(2):
            o_hop(e, way).wait_recv()
            o_pass(e, way).start()

    kv_rows = kvg[...].reshape(z.group, 2 * hd)
    kv_arrive, kv_finish = exchange(
        kv_rows, send_kv, recv_kv, dkv_s, dkv_r, own.at[2 + 2 * z.local]
    )
    finishes = [kv_finish]
    for e in range(z.local):
        q_own(e).wait()
        for peer in peers(nz, c):
            q_one_in(e, peer).wait_recv()
        for way in range(2):
            q_end(e, way).wait_recv()
        q_arrive, q_finish = exchange(
            qg[e].reshape(z.group, hd), send_q.at[e], recv_q.at[e], dq_s.at[e], dq_r.at[e],
            own.at[3 + 2 * z.local + e],
        )
        finishes.append(q_finish)
        if e > 0:
            pass_outputs(e - 1)
        if e + 1 < z.local:
            pass_q_rows(e + 1)
        if e == 0:
            kv_arrive()
            compact(recv_kv, pkv, z.doc_most)
        q_arrive()
        compact(recv_q.at[e], pq, 0)
        run, owners = z.blocks // z.pieces, nz // z.pieces
        home, way = c // owners, 1 + (z.pieces - 2) * lax.rem(c, 2)
        for turn in range(z.pieces):
            step = (z.pieces // 2, way, z.pieces - way, 0)[turn] if z.pieces == 4 else turn
            piece = lax.rem(home + step, z.pieces)
            attend(e, piece * run, run)
            for i in range(owners):
                peer = piece * owners + i

                @pl.when((peer != c) & (peer != facing))
                def _():
                    o_one(e, peer).start()

                @pl.when(peer == facing)
                def _():
                    for way in range(2):
                        o_hop(e, way).start()

                @pl.when(peer == c)
                def _():
                    o_own(e).start()

    pass_outputs(z.local - 1)
    for peer in peers(nz, c) + [facing]:
        for half in range(2):
            kv_one(half, peer).wait_send()
    for e in range(z.local):
        for peer in peers(nz, c):
            q_one(e, peer).wait_send()
        for way in range(2):
            q_hop(e, way).wait_send()
            q_pass(e, way).wait_send()
            o_hop(e, way).wait_send()
            o_pass(e, way).wait_send()
    for k in range(1, z.team):
        kv_two(k).wait_send()
    for finish in finishes:
        finish()
    for e in range(z.local):
        o_own(e).wait()
        for way in range(2):
            o_end(e, way).wait_recv()
        for peer in peers(nz, c):
            o_one_in(e, peer).wait_recv()
        for peer in peers(nz, c):
            o_one(e, peer).wait_send()


def call(z, route, docs, q_src, kv_src):
    hd = HEAD_DIM
    dma = pltpu.SemaphoreType.DMA
    vmem = pltpu.VMEM
    return pl.pallas_call(
        functools.partial(kernel, z),
        out_shape=jax.ShapeDtypeStruct((z.slots, z.heads * hd), BF16),
        in_specs=[
            pl.BlockSpec(memory_space=pltpu.VMEM),
            pl.BlockSpec(memory_space=pltpu.VMEM),
            pl.BlockSpec(memory_space=pl.ANY),
            pl.BlockSpec(memory_space=pl.ANY),
        ],
        out_specs=pl.BlockSpec(memory_space=pl.ANY),
        scratch_shapes=[
            vmem((z.local, z.ctx, z.rows, hd), BF16),
            vmem((z.ctx, z.team, z.part, 2 * hd), BF16),
            vmem((z.local, z.pack, hd), BF16),
            vmem((z.pack, 2 * hd), BF16),
            vmem((z.local, z.pack, hd), BF16),
            vmem((z.pack, 2 * hd), BF16),
            vmem((z.pack, hd), BF16),
            vmem((z.doc_most + z.pack, 2 * hd), BF16),
            vmem((z.local, z.pack, hd), BF16),
            vmem((z.batches, BATCH * z.cap, z.group), BF16),
            vmem((z.pack, z.pack), BF16),
            vmem((z.lanes, 128), I32),
            vmem((z.tiles, 128), I32),
            vmem((z.doc_most // 128 + z.tiles, 128), I32),
            vmem((z.pack, 128), I32),
            vmem((8, 128), I32),
            vmem((z.local, 2, z.rows // 2, hd), BF16),
            vmem((z.local, 2, z.slots // 2, hd), BF16),
            dma((2, z.local, 2)),
            dma((2, z.local, 2)),
            dma((2, z.local, 2)),
            dma((2, z.local, 2)),
            dma((z.local, z.ctx)),
            dma((z.local, z.ctx)),
            dma((2, z.ctx)),
            dma((2, z.ctx)),
            dma((z.team,)),
            dma((z.team,)),
            dma((z.dp,)),
            dma((z.dp,)),
            dma((z.local, z.dp)),
            dma((z.local, z.dp)),
            dma((z.local, z.ctx)),
            dma((z.local, z.ctx)),
            dma((3 + 3 * z.local,)),
        ],
        compiler_params=pltpu.CompilerParams(
            collective_id=0, has_side_effects=True, vmem_limit_bytes=56 << 20
        ),
    )(route, docs, q_src, kv_src)


def on_device(z, q_src, kv_src, route, doc_ids):
    return call(z, route.reshape(-1, 128), doc_ids.reshape(-1, 128), q_src, kv_src)


def solution(mesh):
    z = Sizes(
        mesh.shape["dp"], mesh.shape["ctx"], 128, 96, Q_HEADS, KV_HEADS, DOC_MOST, BLOCK
    )
    in_specs = (P(("dp", "ctx"), None), P(("dp", "ctx"), None), P(), P("dp", None))
    return jax.shard_map(
        functools.partial(on_device, z),
        mesh=mesh,
        in_specs=in_specs,
        out_specs=P(("dp", "ctx"), None),
        check_vma=False,
    )
```

```python
import functools
import math

import jax
import jax.numpy as jnp
from jax import lax
from jax.experimental import pallas as pl
from jax.experimental.pallas import tpu as pltpu
from jax.sharding import PartitionSpec as P

Q_HEADS = 32
KV_HEADS = 4
HEAD_DIM = 128
DOC_MOST = 1024
BLOCK = 256
BATCH = 4
NEG = -1e30
MESH = pl.DeviceIdType.MESH
BF16 = jnp.bfloat16
F32 = jnp.float32
I32 = jnp.int32


class Sizes:
    def __init__(self, dp, ctx, rows, cap, heads, kv_heads, doc_most, block):
        self.dp, self.ctx, self.rows, self.cap = dp, ctx, rows, cap
        self.heads, self.kv_heads = heads, kv_heads
        self.local = heads // ctx
        self.team = ctx // kv_heads
        self.group = rows * ctx
        self.pack = dp * cap
        self.slots = self.pack // ctx
        self.part = rows // self.team
        self.lanes = self.group // 128
        self.tiles = self.pack // 128
        self.doc_most, self.block = doc_most, block
        self.blocks = self.pack // block
        self.window = doc_most + block
        self.batches = dp // BATCH
        self.span = math.gcd(self.pack, 2 * block)
        self.pieces = math.gcd(self.blocks, 4)


def iota(shape, dim):
    return lax.broadcasted_iota(I32, shape, dim)


def alternating(n):
    order = []
    for k in range(n // 2 - 1, 0, -1):
        order += [k, n - k]
    return order


def kernel(
    z, route_ref, doc_ref, q_hbm, kv_hbm, out_ref,
    qg, kvg, send_q, send_kv, recv_q, recv_kv, pq, pkv, ob, pick, place,
    target, pos, key_doc, query_doc, live_col, relay_q, relay_o,
    hop_s, hop_r, end_s, end_r, zq_s, zq_r, k1_s, k1_r, k2_s, k2_r, dkv_s, dkv_r, dq_s, dq_r, o_s, o_r, own,
):
    g = lax.axis_index("dp")
    c = lax.axis_index("ctx")
    nz, nd, hd = z.ctx, z.dp, HEAD_DIM
    quarter = lax.rem(c, z.team)
    quad = c - quarter

    barrier = pltpu.get_barrier_semaphore()

    def greet(axis, me, n):
        def body(k, _):
            pl.semaphore_signal(
                barrier, inc=1, device_id={axis: lax.rem(me + k, n)}, device_id_type=MESH
            )
            return 0

        lax.fori_loop(1, n, body, 0)

    greet("ctx", c, nz)
    greet("dp", g, nd)
    pl.semaphore_wait(barrier, nz + nd - 2)

    def remote(src, dst, s, r, axis, peer):
        return pltpu.make_async_remote_copy(
            src_ref=src, dst_ref=dst, send_sem=s, recv_sem=r,
            device_id={axis: peer}, device_id_type=MESH,
        )

    def kv_cut(half, peer):
        part = lax.rem(peer, z.team)
        head = peer // z.team
        rows = pl.ds(pl.multiple_of(part * z.part, z.part), z.part)
        cols = pl.ds(pl.multiple_of((half * z.kv_heads + head) * hd, hd), hd)
        return kv_hbm.at[rows, cols], part

    def kv_one(half, peer):
        src, part = kv_cut(half, peer)
        dst = kvg.at[c, part, :, pl.ds(half * hd, hd)]
        return remote(src, dst, k1_s.at[half, peer], k1_r.at[half, c], "ctx", peer)

    def kv_one_in(half, peer):
        dst = kvg.at[peer, quarter, :, pl.ds(half * hd, hd)]
        return remote(dst, dst, k1_s.at[half, peer], k1_r.at[half, peer], "ctx", peer)

    def kv_own(half):
        src, part = kv_cut(half, c)
        return pltpu.make_async_copy(
            src, kvg.at[c, part, :, pl.ds(half * hd, hd)], own.at[half]
        )

    def q_cut(e, peer):
        return q_hbm.at[:, pl.ds(pl.multiple_of((peer * z.local + e) * hd, hd), hd)]

    def q_one(e, peer):
        return remote(q_cut(e, peer), qg.at[e, c], zq_s.at[e, peer], zq_r.at[e, c], "ctx", peer)

    def q_one_in(e, peer):
        dst = qg.at[e, peer]
        return remote(dst, dst, zq_s.at[e, peer], zq_r.at[e, peer], "ctx", peer)

    def q_own(e):
        return pltpu.make_async_copy(q_cut(e, c), qg.at[e, c], own.at[2 + e])

    def peers(n, me):
        return [lax.rem(me + k, n) for k in alternating(n)]

    facing = lax.rem(c + nz // 2, nz)
    turns = (nz // 4, nz - nz // 4)

    def half_of(ref, way, n):
        return ref.at[pl.ds(way * (n // 2), n // 2)]

    def hop(block, relay, kind, e, way):
        peer = lax.rem(c + turns[way], nz)
        return remote(
            block, relay.at[e, way], hop_s.at[kind, e, way], hop_r.at[kind, e, way], "ctx", peer
        )

    def hand_on(relay, dst, kind, e, way):
        peer = lax.rem(c + turns[way], nz)
        return remote(
            relay.at[e, way], dst, end_s.at[kind, e, way], end_r.at[kind, e, way], "ctx", peer
        )

    def q_hop(e, way):
        return hop(half_of(q_cut(e, facing), way, z.rows), relay_q, 0, e, way)

    def q_pass(e, way):
        origin = lax.rem(c + turns[1 - way], nz)
        return hand_on(relay_q, half_of(qg.at[e, origin], way, z.rows), 0, e, way)

    def q_end(e, way):
        return hand_on(relay_q, half_of(qg.at[e, facing], way, z.rows), 0, e, way)

    def send_q_rows(e):
        for way in range(2):
            q_hop(e, way).start()
        for peer in peers(nz, c):
            q_one(e, peer).start()
        q_own(e).start()

    def pass_q_rows(e):
        for way in range(2):
            q_hop(e, way).wait_recv()
            q_pass(e, way).start()

    for peer in peers(nz, c) + [facing]:
        for half in range(2):
            kv_one(half, peer).start()
    for half in range(2):
        kv_own(half).start()

    lane = iota((1, 128), 1)
    plan = route_ref[pl.ds(pl.multiple_of(g * z.lanes, z.lanes), z.lanes), :]
    upper = (iota((128, 128), 0) < iota((128, 128), 1)).astype(F32).astype(BF16)
    running = jnp.zeros((nd, 1), F32)
    for i in range(z.lanes):
        mine = (plan[i : i + 1, :] == iota((nd, 128), 0)).astype(F32)
        before = jnp.dot(mine.astype(BF16), upper, preferred_element_type=F32) + running
        rank = jnp.sum(mine * before, axis=0, keepdims=True)
        target[i : i + 1, :] = plan[i : i + 1, :] * z.cap + rank.astype(I32)
        running = running + jnp.sum(mine, axis=1, keepdims=True)

    def pick_batch(j, _):
        first = j * (BATCH * z.cap)
        rows = iota((BATCH * z.cap, 128), 0) + first
        for i in range(z.lanes):
            hit = rows == target[i : i + 1, :]
            pick[j, :, i * 128 : (i + 1) * 128] = jnp.where(hit, 1.0, 0.0).astype(BF16)
        return 0

    lax.fori_loop(0, z.batches, pick_batch, 0)

    for half in range(2):
        kv_own(half).wait()
    for peer in peers(nz, c) + [facing]:
        for half in range(2):
            kv_one_in(half, peer).wait_recv()

    def kv_two(k):
        other = lax.rem(quarter + k, z.team)
        block = kvg.at[:, quarter]
        return remote(block, block, k2_s.at[k], k2_r.at[k], "ctx", quad + other)

    def kv_two_in(k):
        other = lax.rem(quarter - k + z.team, z.team)
        block = kvg.at[:, other]
        return remote(block, block, k2_s.at[k], k2_r.at[k], "ctx", quad + other)

    for k in range(1, z.team):
        kv_two(k).start()
    arriving = (route_ref[...] == g).astype(F32)
    tally = jnp.sum(arriving.reshape(nd, z.lanes, 128), axis=1)
    count = jnp.sum(tally, axis=1, keepdims=True)
    lower = (iota((nd, nd), 1) < iota((nd, nd), 0)).astype(F32).astype(BF16)
    start = jnp.sum(
        jnp.dot(lower, tally.astype(BF16), preferred_element_type=F32), axis=1, keepdims=True
    )
    live_col[...] = jnp.broadcast_to(jnp.sum(count, axis=0, keepdims=True), (8, 128)).astype(I32)
    count, start = count.astype(I32), start.astype(I32)
    for i in range(z.tiles):
        offset = iota((nd, 128), 1) + i * 128 - z.cap * iota((nd, 128), 0)
        held = (offset >= 0) & (offset < z.cap) & (offset < count)
        slot = jnp.sum(jnp.where(held, (start + offset + 1).astype(F32), 0.0), axis=0, keepdims=True)
        pos[i : i + 1, :] = slot.astype(I32) - 1

    per = z.block // 128

    def place_row(b, _):
        rows = iota((z.span, 128), 0) + b * z.span

        def place_one(k, _):
            hit = rows == pos[pl.ds(k, 1), :]
            cols = pl.ds(pl.multiple_of(k * 128, 128), 128)
            place[pl.ds(pl.multiple_of(b * z.span, z.span), z.span), cols] = jnp.where(
                hit, 1.0, 0.0
            ).astype(BF16)
            return 0

        return lax.fori_loop(b * (z.span // 128), z.tiles, place_one, 0)

    lax.fori_loop(0, z.pack // z.span, place_row, 0)

    lead = z.doc_most // 128
    key_doc[0:lead, :] = jnp.full((lead, 128), -1, I32)
    key_doc[lead : lead + z.tiles, :] = doc_ref[...]
    for i in range(z.tiles):
        row = jnp.broadcast_to(doc_ref[i : i + 1, :].astype(F32), (128, 128))
        query_doc[i * 128 : (i + 1) * 128, :] = row.T.astype(I32)
    pkv[0 : z.doc_most, :] = jnp.zeros((z.doc_most, 2 * hd), BF16)

    for k in range(1, z.team):
        kv_two_in(k).wait_recv()
    send_q_rows(0)

    def exchange(rows, send, recv, send_sem, recv_sem, own_sem):
        first = g // BATCH

        def rows_of(ref, s):
            return ref.at[pl.ds(pl.multiple_of(s * z.cap, z.cap), z.cap)]

        def leave(s):
            return remote(rows_of(send, s), rows_of(recv, g), send_sem.at[s], recv_sem.at[g], "dp", s)

        def stay():
            return pltpu.make_async_copy(rows_of(send, g), rows_of(recv, g), own_sem)

        def body(j, _):
            j = lax.rem(first + j, z.batches)
            block = jnp.dot(pick[j], rows, preferred_element_type=F32).astype(BF16)
            height = BATCH * z.cap
            send[pl.ds(pl.multiple_of(j * height, height), height), :] = block
            for i in range(BATCH):
                s = j * BATCH + i

                @pl.when(s != g)
                def _():
                    leave(s).start()

                @pl.when(s == g)
                def _():
                    stay().start()

            return 0

        lax.fori_loop(0, z.batches, body, 0)

        def arrive():
            def body(k, _):
                s = lax.rem(g + k, nd)
                block = rows_of(recv, s)
                remote(block, block, send_sem.at[s], recv_sem.at[s], "dp", s).wait_recv()
                return 0

            stay().wait()
            lax.fori_loop(1, nd, body, 0)

        def finish():
            def body(k, _):
                leave(lax.rem(g + k, nd)).wait_send()
                return 0

            lax.fori_loop(1, nd, body, 0)

        return arrive, finish

    def compact(recv, dst, base):
        for b in range(0, z.pack, z.span):
            rows = jnp.dot(
                place[b : b + z.span, b : z.pack], recv[b : z.pack, :], preferred_element_type=F32
            )
            dst[base + b : base + b + z.span, :] = rows.astype(BF16)

    factor = float(hd**-0.5 * 1.4426950408889634)
    wide = z.window // 128

    def attend(e, first, count):
        def body(b, _):
            at = pl.multiple_of(b * z.block, z.block)
            queries = pq[pl.ds(at, z.block), :]
            keys = pkv[pl.ds(at, z.window), 0:hd]
            scores = lax.dot_general(
                queries, keys, (((1,), (1,)), ((), ())), preferred_element_type=F32
            )
            own_doc = query_doc[pl.ds(at, z.block), :]
            cuts = []
            for i in range(wide):
                ok = own_doc == key_doc[pl.ds(b * per + i, 1), :]
                j = i - (wide - per)
                if j >= 0:
                    ok = ok & (iota((z.block, 128), 1) + j * 128 <= iota((z.block, 128), 0))
                cuts.append(jnp.where(ok, scores[:, i * 128 : (i + 1) * 128], NEG))
            masked = jnp.concatenate(cuts, axis=1)
            top = jnp.max(masked, axis=1, keepdims=True)
            exponent = jnp.exp2((masked - top) * factor)
            total = jnp.sum(exponent, axis=1, keepdims=True)
            values = pkv[pl.ds(at, z.window), hd : 2 * hd]
            mixed = jnp.dot(exponent.astype(BF16), values, preferred_element_type=F32) / total
            alive = iota((z.block, hd), 0) + at < live_col[0:1, :]
            ob[e, pl.ds(at, z.block), :] = jnp.where(alive, mixed, 0.0).astype(BF16)
            return 0

        lax.fori_loop(first, first + count, body, 0)

    def out_cols(peer, e):
        return pl.ds(pl.multiple_of((peer * z.local + e) * hd, hd), hd)

    def out_rows(peer, e):
        return ob.at[e, pl.ds(pl.multiple_of(peer * z.slots, z.slots), z.slots)]

    def o_one(e, peer):
        dst = out_ref.at[:, out_cols(c, e)]
        return remote(out_rows(peer, e), dst, o_s.at[e, peer], o_r.at[e, c], "ctx", peer)

    def o_one_in(e, peer):
        dst = out_ref.at[:, out_cols(peer, e)]
        return remote(out_rows(peer, e), dst, o_s.at[e, peer], o_r.at[e, peer], "ctx", peer)

    def o_own(e):
        return pltpu.make_async_copy(
            out_rows(c, e), out_ref.at[:, out_cols(c, e)], own.at[2 + z.local + e]
        )

    def o_hop(e, way):
        return hop(half_of(out_rows(facing, e), way, z.slots), relay_o, 1, e, way)

    def o_pass(e, way):
        origin = lax.rem(c + turns[1 - way], nz)
        dst = half_of(out_ref, way, z.slots).at[:, out_cols(origin, e)]
        return hand_on(relay_o, dst, 1, e, way)

    def o_end(e, way):
        dst = half_of(out_ref, way, z.slots).at[:, out_cols(facing, e)]
        return hand_on(relay_o, dst, 1, e, way)

    def pass_outputs(e):
        for way in range(2):
            o_hop(e, way).wait_recv()
            o_pass(e, way).start()

    kv_rows = kvg[...].reshape(z.group, 2 * hd)
    kv_arrive, kv_finish = exchange(
        kv_rows, send_kv, recv_kv, dkv_s, dkv_r, own.at[2 + 2 * z.local]
    )
    finishes = [kv_finish]
    pass_q_rows(0)
    for e in range(z.local):
        q_own(e).wait()
        for peer in peers(nz, c):
            q_one_in(e, peer).wait_recv()
        for way in range(2):
            q_end(e, way).wait_recv()
        if e + 1 < z.local:
            send_q_rows(e + 1)
        q_arrive, q_finish = exchange(
            qg[e].reshape(z.group, hd), send_q.at[e], recv_q.at[e], dq_s.at[e], dq_r.at[e],
            own.at[3 + 2 * z.local + e],
        )
        finishes.append(q_finish)
        if e > 0:
            pass_outputs(e - 1)
        if e == 0:
            kv_arrive()
            compact(recv_kv, pkv, z.doc_most)
        q_arrive()
        if e + 1 < z.local:
            pass_q_rows(e + 1)
        compact(recv_q.at[e], pq, 0)
        run, owners = z.blocks // z.pieces, nz // z.pieces
        home, way = c // owners, 1 + (z.pieces - 2) * lax.rem(c, 2)
        for turn in range(z.pieces):
            step = (z.pieces // 2, way, z.pieces - way, 0)[turn] if z.pieces == 4 else turn
            piece = lax.rem(home + step, z.pieces)
            attend(e, piece * run, run)
            for i in range(owners):
                peer = piece * owners + i

                @pl.when((peer != c) & (peer != facing))
                def _():
                    o_one(e, peer).start()

                @pl.when(peer == facing)
                def _():
                    for way in range(2):
                        o_hop(e, way).start()

                @pl.when(peer == c)
                def _():
                    o_own(e).start()

    pass_outputs(z.local - 1)
    for peer in peers(nz, c) + [facing]:
        for half in range(2):
            kv_one(half, peer).wait_send()
    for e in range(z.local):
        for peer in peers(nz, c):
            q_one(e, peer).wait_send()
        for way in range(2):
            q_hop(e, way).wait_send()
            q_pass(e, way).wait_send()
            o_hop(e, way).wait_send()
            o_pass(e, way).wait_send()
    for k in range(1, z.team):
        kv_two(k).wait_send()
    for finish in finishes:
        finish()
    for e in range(z.local):
        o_own(e).wait()
        for way in range(2):
            o_end(e, way).wait_recv()
        for peer in peers(nz, c):
            o_one_in(e, peer).wait_recv()
        for peer in peers(nz, c):
            o_one(e, peer).wait_send()


def call(z, route, docs, q_src, kv_src):
    hd = HEAD_DIM
    dma = pltpu.SemaphoreType.DMA
    vmem = pltpu.VMEM
    return pl.pallas_call(
        functools.partial(kernel, z),
        out_shape=jax.ShapeDtypeStruct((z.slots, z.heads * hd), BF16),
        in_specs=[
            pl.BlockSpec(memory_space=pltpu.VMEM),
            pl.BlockSpec(memory_space=pltpu.VMEM),
            pl.BlockSpec(memory_space=pl.ANY),
            pl.BlockSpec(memory_space=pl.ANY),
        ],
        out_specs=pl.BlockSpec(memory_space=pl.ANY),
        scratch_shapes=[
            vmem((z.local, z.ctx, z.rows, hd), BF16),
            vmem((z.ctx, z.team, z.part, 2 * hd), BF16),
            vmem((z.local, z.pack, hd), BF16),
            vmem((z.pack, 2 * hd), BF16),
            vmem((z.local, z.pack, hd), BF16),
            vmem((z.pack, 2 * hd), BF16),
            vmem((z.pack, hd), BF16),
            vmem((z.doc_most + z.pack, 2 * hd), BF16),
            vmem((z.local, z.pack, hd), BF16),
            vmem((z.batches, BATCH * z.cap, z.group), BF16),
            vmem((z.pack, z.pack), BF16),
            vmem((z.lanes, 128), I32),
            vmem((z.tiles, 128), I32),
            vmem((z.doc_most // 128 + z.tiles, 128), I32),
            vmem((z.pack, 128), I32),
            vmem((8, 128), I32),
            vmem((z.local, 2, z.rows // 2, hd), BF16),
            vmem((z.local, 2, z.slots // 2, hd), BF16),
            dma((2, z.local, 2)),
            dma((2, z.local, 2)),
            dma((2, z.local, 2)),
            dma((2, z.local, 2)),
            dma((z.local, z.ctx)),
            dma((z.local, z.ctx)),
            dma((2, z.ctx)),
            dma((2, z.ctx)),
            dma((z.team,)),
            dma((z.team,)),
            dma((z.dp,)),
            dma((z.dp,)),
            dma((z.local, z.dp)),
            dma((z.local, z.dp)),
            dma((z.local, z.ctx)),
            dma((z.local, z.ctx)),
            dma((3 + 3 * z.local,)),
        ],
        compiler_params=pltpu.CompilerParams(
            collective_id=0, has_side_effects=True, vmem_limit_bytes=56 << 20
        ),
    )(route, docs, q_src, kv_src)


def on_device(z, q_src, kv_src, route, doc_ids):
    return call(z, route.reshape(-1, 128), doc_ids.reshape(-1, 128), q_src, kv_src)


def solution(mesh):
    z = Sizes(
        mesh.shape["dp"], mesh.shape["ctx"], 128, 96, Q_HEADS, KV_HEADS, DOC_MOST, BLOCK
    )
    in_specs = (P(("dp", "ctx"), None), P(("dp", "ctx"), None), P(), P("dp", None))
    return jax.shard_map(
        functools.partial(on_device, z),
        mesh=mesh,
        in_specs=in_specs,
        out_specs=P(("dp", "ctx"), None),
        check_vma=False,
    )
```

```python
import functools
import math

import jax
import jax.numpy as jnp
from jax import lax
from jax.experimental import pallas as pl
from jax.experimental.pallas import tpu as pltpu
from jax.sharding import PartitionSpec as P

Q_HEADS = 32
KV_HEADS = 4
HEAD_DIM = 128
DOC_MOST = 1024
BLOCK = 256
BATCH = 4
NEG = -1e30
MESH = pl.DeviceIdType.MESH
BF16 = jnp.bfloat16
F32 = jnp.float32
I32 = jnp.int32


class Sizes:
    def __init__(self, dp, ctx, rows, cap, heads, kv_heads, doc_most, block):
        self.dp, self.ctx, self.rows, self.cap = dp, ctx, rows, cap
        self.heads, self.kv_heads = heads, kv_heads
        self.local = heads // ctx
        self.team = ctx // kv_heads
        self.group = rows * ctx
        self.pack = dp * cap
        self.slots = self.pack // ctx
        self.part = rows // self.team
        self.lanes = self.group // 128
        self.tiles = self.pack // 128
        self.doc_most, self.block = doc_most, block
        self.blocks = self.pack // block
        self.window = doc_most + block
        self.batches = dp // BATCH
        self.span = math.gcd(self.pack, 2 * block)
        self.pieces = math.gcd(self.blocks, 4)


def iota(shape, dim):
    return lax.broadcasted_iota(I32, shape, dim)


def alternating(n):
    order = []
    for k in range(n // 2 - 1, 0, -1):
        order += [k, n - k]
    return order


def kernel(
    z, route_ref, doc_ref, q_hbm, kv_hbm, out_ref,
    qg, kvg, send_q, send_kv, recv_q, recv_kv, pq, pkv, ob, pick, place,
    target, pos, key_doc, query_doc, live_col, relay_q, relay_o,
    hop_s, hop_r, end_s, end_r, zq_s, zq_r, k1_s, k1_r, k2_s, k2_r, dkv_s, dkv_r, dq_s, dq_r, o_s, o_r, own,
):
    g = lax.axis_index("dp")
    c = lax.axis_index("ctx")
    nz, nd, hd = z.ctx, z.dp, HEAD_DIM
    quarter = lax.rem(c, z.team)
    quad = c - quarter

    barrier = pltpu.get_barrier_semaphore()

    def greet(axis, me, n):
        def body(k, _):
            pl.semaphore_signal(
                barrier, inc=1, device_id={axis: lax.rem(me + k, n)}, device_id_type=MESH
            )
            return 0

        lax.fori_loop(1, n, body, 0)

    greet("ctx", c, nz)
    greet("dp", g, nd)
    pl.semaphore_wait(barrier, nz + nd - 2)

    def remote(src, dst, s, r, axis, peer):
        return pltpu.make_async_remote_copy(
            src_ref=src, dst_ref=dst, send_sem=s, recv_sem=r,
            device_id={axis: peer}, device_id_type=MESH,
        )

    def kv_cut(half, peer):
        part = lax.rem(peer, z.team)
        head = peer // z.team
        rows = pl.ds(pl.multiple_of(part * z.part, z.part), z.part)
        cols = pl.ds(pl.multiple_of((half * z.kv_heads + head) * hd, hd), hd)
        return kv_hbm.at[rows, cols], part

    def kv_one(half, peer):
        src, part = kv_cut(half, peer)
        dst = kvg.at[c, part, :, pl.ds(half * hd, hd)]
        return remote(src, dst, k1_s.at[half, peer], k1_r.at[half, c], "ctx", peer)

    def kv_one_in(half, peer):
        dst = kvg.at[peer, quarter, :, pl.ds(half * hd, hd)]
        return remote(dst, dst, k1_s.at[half, peer], k1_r.at[half, peer], "ctx", peer)

    def kv_own(half):
        src, part = kv_cut(half, c)
        return pltpu.make_async_copy(
            src, kvg.at[c, part, :, pl.ds(half * hd, hd)], own.at[half]
        )

    def q_cut(e, peer):
        return q_hbm.at[:, pl.ds(pl.multiple_of((peer * z.local + e) * hd, hd), hd)]

    def q_one(e, peer):
        return remote(q_cut(e, peer), qg.at[e, c], zq_s.at[e, peer], zq_r.at[e, c], "ctx", peer)

    def q_one_in(e, peer):
        dst = qg.at[e, peer]
        return remote(dst, dst, zq_s.at[e, peer], zq_r.at[e, peer], "ctx", peer)

    def q_own(e):
        return pltpu.make_async_copy(q_cut(e, c), qg.at[e, c], own.at[2 + e])

    def peers(n, me):
        return [lax.rem(me + k, n) for k in alternating(n)]

    facing = lax.rem(c + nz // 2, nz)
    turns = (nz // 4, nz - nz // 4)

    def half_of(ref, way, n):
        return ref.at[pl.ds(way * (n // 2), n // 2)]

    def hop(block, relay, kind, e, way):
        peer = lax.rem(c + turns[way], nz)
        return remote(
            block, relay.at[e, way], hop_s.at[kind, e, way], hop_r.at[kind, e, way], "ctx", peer
        )

    def hand_on(relay, dst, kind, e, way):
        peer = lax.rem(c + turns[way], nz)
        return remote(
            relay.at[e, way], dst, end_s.at[kind, e, way], end_r.at[kind, e, way], "ctx", peer
        )

    def q_hop(e, way):
        return hop(half_of(q_cut(e, facing), way, z.rows), relay_q, 0, e, way)

    def q_pass(e, way):
        origin = lax.rem(c + turns[1 - way], nz)
        return hand_on(relay_q, half_of(qg.at[e, origin], way, z.rows), 0, e, way)

    def q_end(e, way):
        return hand_on(relay_q, half_of(qg.at[e, facing], way, z.rows), 0, e, way)

    def send_q_rows(e):
        for way in range(2):
            q_hop(e, way).start()
        for peer in peers(nz, c):
            q_one(e, peer).start()
        q_own(e).start()

    def pass_q_rows(e):
        for way in range(2):
            q_hop(e, way).wait_recv()
            q_pass(e, way).start()

    for peer in peers(nz, c) + [facing]:
        for half in range(2):
            kv_one(half, peer).start()
    for half in range(2):
        kv_own(half).start()

    lane = iota((1, 128), 1)
    plan = route_ref[pl.ds(pl.multiple_of(g * z.lanes, z.lanes), z.lanes), :]
    upper = (iota((128, 128), 0) < iota((128, 128), 1)).astype(F32).astype(BF16)
    running = jnp.zeros((nd, 1), F32)
    for i in range(z.lanes):
        mine = (plan[i : i + 1, :] == iota((nd, 128), 0)).astype(F32)
        before = jnp.dot(mine.astype(BF16), upper, preferred_element_type=F32) + running
        rank = jnp.sum(mine * before, axis=0, keepdims=True)
        target[i : i + 1, :] = plan[i : i + 1, :] * z.cap + rank.astype(I32)
        running = running + jnp.sum(mine, axis=1, keepdims=True)

    def pick_batch(j, _):
        first = j * (BATCH * z.cap)
        rows = iota((BATCH * z.cap, 128), 0) + first
        for i in range(z.lanes):
            hit = rows == target[i : i + 1, :]
            pick[j, :, i * 128 : (i + 1) * 128] = jnp.where(hit, 1.0, 0.0).astype(BF16)
        return 0

    lax.fori_loop(0, z.batches, pick_batch, 0)

    for half in range(2):
        kv_own(half).wait()
    for peer in peers(nz, c) + [facing]:
        for half in range(2):
            kv_one_in(half, peer).wait_recv()

    def kv_two(k):
        other = lax.rem(quarter + k, z.team)
        block = kvg.at[:, quarter]
        return remote(block, block, k2_s.at[k], k2_r.at[k], "ctx", quad + other)

    def kv_two_in(k):
        other = lax.rem(quarter - k + z.team, z.team)
        block = kvg.at[:, other]
        return remote(block, block, k2_s.at[k], k2_r.at[k], "ctx", quad + other)

    for k in range(1, z.team):
        kv_two(k).start()
    send_q_rows(0)
    arriving = (route_ref[...] == g).astype(F32)
    tally = jnp.sum(arriving.reshape(nd, z.lanes, 128), axis=1)
    count = jnp.sum(tally, axis=1, keepdims=True)
    lower = (iota((nd, nd), 1) < iota((nd, nd), 0)).astype(F32).astype(BF16)
    start = jnp.sum(
        jnp.dot(lower, tally.astype(BF16), preferred_element_type=F32), axis=1, keepdims=True
    )
    live_col[...] = jnp.broadcast_to(jnp.sum(count, axis=0, keepdims=True), (8, 128)).astype(I32)
    count, start = count.astype(I32), start.astype(I32)
    for i in range(z.tiles):
        offset = iota((nd, 128), 1) + i * 128 - z.cap * iota((nd, 128), 0)
        held = (offset >= 0) & (offset < z.cap) & (offset < count)
        slot = jnp.sum(jnp.where(held, (start + offset + 1).astype(F32), 0.0), axis=0, keepdims=True)
        pos[i : i + 1, :] = slot.astype(I32) - 1

    per = z.block // 128

    def place_row(b, _):
        rows = iota((z.span, 128), 0) + b * z.span

        def place_one(k, _):
            hit = rows == pos[pl.ds(k, 1), :]
            cols = pl.ds(pl.multiple_of(k * 128, 128), 128)
            place[pl.ds(pl.multiple_of(b * z.span, z.span), z.span), cols] = jnp.where(
                hit, 1.0, 0.0
            ).astype(BF16)
            return 0

        return lax.fori_loop(b * (z.span // 128), z.tiles, place_one, 0)

    lax.fori_loop(0, z.pack // z.span, place_row, 0)

    lead = z.doc_most // 128
    key_doc[0:lead, :] = jnp.full((lead, 128), -1, I32)
    key_doc[lead : lead + z.tiles, :] = doc_ref[...]
    for i in range(z.tiles):
        row = jnp.broadcast_to(doc_ref[i : i + 1, :].astype(F32), (128, 128))
        query_doc[i * 128 : (i + 1) * 128, :] = row.T.astype(I32)
    pkv[0 : z.doc_most, :] = jnp.zeros((z.doc_most, 2 * hd), BF16)

    for k in range(1, z.team):
        kv_two_in(k).wait_recv()
    pass_q_rows(0)

    def exchange(rows, send, recv, send_sem, recv_sem, own_sem):
        first = g // BATCH

        def rows_of(ref, s):
            return ref.at[pl.ds(pl.multiple_of(s * z.cap, z.cap), z.cap)]

        def leave(s):
            return remote(rows_of(send, s), rows_of(recv, g), send_sem.at[s], recv_sem.at[g], "dp", s)

        def stay():
            return pltpu.make_async_copy(rows_of(send, g), rows_of(recv, g), own_sem)

        def body(j, _):
            j = lax.rem(first + j, z.batches)
            block = jnp.dot(pick[j], rows, preferred_element_type=F32).astype(BF16)
            height = BATCH * z.cap
            send[pl.ds(pl.multiple_of(j * height, height), height), :] = block
            for i in range(BATCH):
                s = j * BATCH + i

                @pl.when(s != g)
                def _():
                    leave(s).start()

                @pl.when(s == g)
                def _():
                    stay().start()

            return 0

        lax.fori_loop(0, z.batches, body, 0)

        def arrive():
            def body(k, _):
                s = lax.rem(g + k, nd)
                block = rows_of(recv, s)
                remote(block, block, send_sem.at[s], recv_sem.at[s], "dp", s).wait_recv()
                return 0

            stay().wait()
            lax.fori_loop(1, nd, body, 0)

        def finish():
            def body(k, _):
                leave(lax.rem(g + k, nd)).wait_send()
                return 0

            lax.fori_loop(1, nd, body, 0)

        return arrive, finish

    def compact(recv, dst, base):
        for b in range(0, z.pack, z.span):
            rows = jnp.dot(
                place[b : b + z.span, b : z.pack], recv[b : z.pack, :], preferred_element_type=F32
            )
            dst[base + b : base + b + z.span, :] = rows.astype(BF16)

    factor = float(hd**-0.5 * 1.4426950408889634)
    wide = z.window // 128

    def attend(e, first, count):
        def body(b, _):
            at = pl.multiple_of(b * z.block, z.block)
            queries = pq[pl.ds(at, z.block), :]
            keys = pkv[pl.ds(at, z.window), 0:hd]
            scores = lax.dot_general(
                queries, keys, (((1,), (1,)), ((), ())), preferred_element_type=F32
            )
            own_doc = query_doc[pl.ds(at, z.block), :]
            cuts = []
            for i in range(wide):
                ok = own_doc == key_doc[pl.ds(b * per + i, 1), :]
                j = i - (wide - per)
                if j >= 0:
                    ok = ok & (iota((z.block, 128), 1) + j * 128 <= iota((z.block, 128), 0))
                cuts.append(jnp.where(ok, scores[:, i * 128 : (i + 1) * 128], NEG))
            masked = jnp.concatenate(cuts, axis=1)
            top = jnp.max(masked, axis=1, keepdims=True)
            exponent = jnp.exp2((masked - top) * factor)
            total = jnp.sum(exponent, axis=1, keepdims=True)
            values = pkv[pl.ds(at, z.window), hd : 2 * hd]
            mixed = jnp.dot(exponent.astype(BF16), values, preferred_element_type=F32) / total
            alive = iota((z.block, hd), 0) + at < live_col[0:1, :]
            ob[e, pl.ds(at, z.block), :] = jnp.where(alive, mixed, 0.0).astype(BF16)
            return 0

        lax.fori_loop(first, first + count, body, 0)

    def out_cols(peer, e):
        return pl.ds(pl.multiple_of((peer * z.local + e) * hd, hd), hd)

    def out_rows(peer, e):
        return ob.at[e, pl.ds(pl.multiple_of(peer * z.slots, z.slots), z.slots)]

    def o_one(e, peer):
        dst = out_ref.at[:, out_cols(c, e)]
        return remote(out_rows(peer, e), dst, o_s.at[e, peer], o_r.at[e, c], "ctx", peer)

    def o_one_in(e, peer):
        dst = out_ref.at[:, out_cols(peer, e)]
        return remote(out_rows(peer, e), dst, o_s.at[e, peer], o_r.at[e, peer], "ctx", peer)

    def o_own(e):
        return pltpu.make_async_copy(
            out_rows(c, e), out_ref.at[:, out_cols(c, e)], own.at[2 + z.local + e]
        )

    def o_hop(e, way):
        return hop(half_of(out_rows(facing, e), way, z.slots), relay_o, 1, e, way)

    def o_pass(e, way):
        origin = lax.rem(c + turns[1 - way], nz)
        dst = half_of(out_ref, way, z.slots).at[:, out_cols(origin, e)]
        return hand_on(relay_o, dst, 1, e, way)

    def o_end(e, way):
        dst = half_of(out_ref, way, z.slots).at[:, out_cols(facing, e)]
        return hand_on(relay_o, dst, 1, e, way)

    def pass_outputs(e):
        for way in range(2):
            o_hop(e, way).wait_recv()
            o_pass(e, way).start()

    kv_rows = kvg[...].reshape(z.group, 2 * hd)
    kv_arrive, kv_finish = exchange(
        kv_rows, send_kv, recv_kv, dkv_s, dkv_r, own.at[2 + 2 * z.local]
    )
    finishes = [kv_finish]
    for e in range(z.local):
        q_own(e).wait()
        for peer in peers(nz, c):
            q_one_in(e, peer).wait_recv()
        for way in range(2):
            q_end(e, way).wait_recv()
        if e + 1 < z.local:
            send_q_rows(e + 1)
        q_arrive, q_finish = exchange(
            qg[e].reshape(z.group, hd), send_q.at[e], recv_q.at[e], dq_s.at[e], dq_r.at[e],
            own.at[3 + 2 * z.local + e],
        )
        finishes.append(q_finish)
        if e > 0:
            pass_outputs(e - 1)
        if e == 0:
            kv_arrive()
            compact(recv_kv, pkv, z.doc_most)
        q_arrive()
        if e + 1 < z.local:
            pass_q_rows(e + 1)
        compact(recv_q.at[e], pq, 0)
        run, owners = z.blocks // z.pieces, nz // z.pieces
        home, way = c // owners, 1 + (z.pieces - 2) * lax.rem(c, 2)
        for turn in range(z.pieces):
            step = (z.pieces // 2, way, z.pieces - way, 0)[turn] if z.pieces == 4 else turn
            piece = lax.rem(home + step, z.pieces)
            attend(e, piece * run, run)
            for i in range(owners):
                peer = piece * owners + i

                @pl.when((peer != c) & (peer != facing))
                def _():
                    o_one(e, peer).start()

                @pl.when(peer == facing)
                def _():
                    for way in range(2):
                        o_hop(e, way).start()

                @pl.when(peer == c)
                def _():
                    o_own(e).start()

    pass_outputs(z.local - 1)
    for peer in peers(nz, c) + [facing]:
        for half in range(2):
            kv_one(half, peer).wait_send()
    for e in range(z.local):
        for peer in peers(nz, c):
            q_one(e, peer).wait_send()
        for way in range(2):
            q_hop(e, way).wait_send()
            q_pass(e, way).wait_send()
            o_hop(e, way).wait_send()
            o_pass(e, way).wait_send()
    for k in range(1, z.team):
        kv_two(k).wait_send()
    for finish in finishes:
        finish()
    for e in range(z.local):
        o_own(e).wait()
        for way in range(2):
            o_end(e, way).wait_recv()
        for peer in peers(nz, c):
            o_one_in(e, peer).wait_recv()
        for peer in peers(nz, c):
            o_one(e, peer).wait_send()


def call(z, route, docs, q_src, kv_src):
    hd = HEAD_DIM
    dma = pltpu.SemaphoreType.DMA
    vmem = pltpu.VMEM
    return pl.pallas_call(
        functools.partial(kernel, z),
        out_shape=jax.ShapeDtypeStruct((z.slots, z.heads * hd), BF16),
        in_specs=[
            pl.BlockSpec(memory_space=pltpu.VMEM),
            pl.BlockSpec(memory_space=pltpu.VMEM),
            pl.BlockSpec(memory_space=pl.ANY),
            pl.BlockSpec(memory_space=pl.ANY),
        ],
        out_specs=pl.BlockSpec(memory_space=pl.ANY),
        scratch_shapes=[
            vmem((z.local, z.ctx, z.rows, hd), BF16),
            vmem((z.ctx, z.team, z.part, 2 * hd), BF16),
            vmem((z.local, z.pack, hd), BF16),
            vmem((z.pack, 2 * hd), BF16),
            vmem((z.local, z.pack, hd), BF16),
            vmem((z.pack, 2 * hd), BF16),
            vmem((z.pack, hd), BF16),
            vmem((z.doc_most + z.pack, 2 * hd), BF16),
            vmem((z.local, z.pack, hd), BF16),
            vmem((z.batches, BATCH * z.cap, z.group), BF16),
            vmem((z.pack, z.pack), BF16),
            vmem((z.lanes, 128), I32),
            vmem((z.tiles, 128), I32),
            vmem((z.doc_most // 128 + z.tiles, 128), I32),
            vmem((z.pack, 128), I32),
            vmem((8, 128), I32),
            vmem((z.local, 2, z.rows // 2, hd), BF16),
            vmem((z.local, 2, z.slots // 2, hd), BF16),
            dma((2, z.local, 2)),
            dma((2, z.local, 2)),
            dma((2, z.local, 2)),
            dma((2, z.local, 2)),
            dma((z.local, z.ctx)),
            dma((z.local, z.ctx)),
            dma((2, z.ctx)),
            dma((2, z.ctx)),
            dma((z.team,)),
            dma((z.team,)),
            dma((z.dp,)),
            dma((z.dp,)),
            dma((z.local, z.dp)),
            dma((z.local, z.dp)),
            dma((z.local, z.ctx)),
            dma((z.local, z.ctx)),
            dma((3 + 3 * z.local,)),
        ],
        compiler_params=pltpu.CompilerParams(
            collective_id=0, has_side_effects=True, vmem_limit_bytes=56 << 20
        ),
    )(route, docs, q_src, kv_src)


def on_device(z, q_src, kv_src, route, doc_ids):
    return call(z, route.reshape(-1, 128), doc_ids.reshape(-1, 128), q_src, kv_src)


def solution(mesh):
    z = Sizes(
        mesh.shape["dp"], mesh.shape["ctx"], 128, 96, Q_HEADS, KV_HEADS, DOC_MOST, BLOCK
    )
    in_specs = (P(("dp", "ctx"), None), P(("dp", "ctx"), None), P(), P("dp", None))
    return jax.shard_map(
        functools.partial(on_device, z),
        mesh=mesh,
        in_specs=in_specs,
        out_specs=P(("dp", "ctx"), None),
        check_vma=False,
    )
```
